128 devices in a mesh: ao: 32 (over x, y, z_hi), aux: 4 (over z_lo, core).
Axes of the slice: x: 4, y: 4, z: 4 (z_hi: 2, z_lo: 2; z = z_hi * 2 + z_lo), core: 2. Of those that a mesh axis runs over, the one named last changes fastest.
Arguments:
- tensor: bfloat16 [64, 4096, 384], P('aux', 'ao'), may hold values from -0.15625 to 0.15625
- pattern: int32 [64, 96], P('aux', 'ao'), may hold values 0 or 1
- occ_density: bfloat16 [4096, 384], P('ao'), may hold values from -0.3125 to 0.3125
- virt_density: bfloat16 [4096, 384], P('ao'), may hold values from -0.3125 to 0.3125
Outputs:
- polarizability: float32 [64, 64], P('aux')
The draws below stay inside these ranges and needn't reach their ends.
All inputs are finite; a program needn't handle non-finite values. No bound on the sum of `pattern` on one device may be relied on, other than what follows from the above.
Results may differ from the reference program's by a relative error of at most 0.0041.
Values may be sent and summed in bfloat16 or wider, within the bound.
A program may use at most 128 MiB of HBM per device.

```python
import jax
import jax.numpy as jnp
from jax import lax

AB = 128
NBLK = 32
NAO = 4096
NAUX = 64


def set_ends(result, key, least, largest):
    longest = result.shape.index(max(result.shape))
    spots = []
    for shift in (0, 1):
        where = [jax.random.randint(jax.random.fold_in(key, axis), (), 0, length) for axis, length in enumerate(result.shape)]
        where[longest] = (where[longest] + shift) % result.shape[longest]
        spots.append(tuple(where))
    return result.at[spots[0]].set(least).at[spots[1]].set(largest)


def shard_levels(own_key, dims, cuts, least, top_value):
    level, own = 1.0, jax.random.fold_in(own_key, 6)
    for axis_at, shards_of in cuts:
        heights = jnp.exp(jax.random.uniform(jax.random.fold_in(own, axis_at), (shards_of,), jnp.float32, least / len(cuts), top_value / len(cuts)))
        level = level * jnp.repeat(heights, dims[axis_at] // shards_of).reshape([-1 if axis == axis_at else 1 for axis in range(len(dims))])
    return level


def gaussian(key, extent, scale, limit, cuts=(), kind=jnp.bfloat16):
    array = jax.random.normal(key, extent, jnp.float32) * scale
    if len(cuts) > 0:
        array = shard_levels(key, extent, cuts, -0.22, 0.18) * array
    return jnp.clip(array, min=-limit, max=limit).astype(kind)


def setup_inputs(seed: int = 0) -> dict:
    key_list = jax.random.split(jax.random.key(seed), 5)
    return {
        "tensor": gaussian(key_list[0], (NAUX, NAO, 3 * AB), ((5 * AB * NAO) ** -0.25), 0.15625, ((0, 4), (1, 32))),
        "pattern": set_ends((jax.random.randint(key_list[1], (NAUX, 3 * NBLK), 0, 4) < 3).astype(jnp.int32), jax.random.fold_in(key_list[1], 1), 0, 1),
        "occ_density": gaussian(key_list[2], (NAO, 3 * AB), (3 * AB) ** -0.5, 0.3125, ((0, 32),)),
        "virt_density": gaussian(key_list[3], (NAO, 3 * AB), (3 * AB) ** -0.5, 0.3125, ((0, 32),)),
    }


def occ_product(single, occ_blocks):
    pieces = [None] * 5
    for offset_a in range(3):
        shifted = jnp.roll(occ_blocks, -(offset_a - 1), axis=0)
        for offset_b in range(3):
            term = jnp.einsum("lik,lkj->lij", single[:, :, offset_a, :], shifted[:, :, offset_b, :])
            slot = offset_a + offset_b
            pieces[slot] = term if pieces[slot] is None else pieces[slot] + term
    return jnp.stack(pieces, axis=2)


def virt_product(virt_blocks, single):
    pieces = [None] * 5
    for offset_a in range(3):
        shifted = jnp.roll(single, -(offset_a - 1), axis=0)
        for offset_b in range(3):
            term = jnp.einsum("lik,lkj->lij", virt_blocks[:, :, offset_a, :], shifted[:, :, offset_b, :])
            slot = offset_a + offset_b
            pieces[slot] = term if pieces[slot] is None else pieces[slot] + term
    return jnp.stack(pieces, axis=2)


def reference(tensor, pattern, occ_density, virt_density):
    masked = tensor.reshape(NAUX, NBLK, AB, 3, AB) * pattern.reshape(NAUX, NBLK, 1, 3, 1).astype(tensor.dtype)
    occ_blocks = occ_density.astype(jnp.float32).reshape(NBLK, AB, 3, AB)
    virt_blocks = virt_density.astype(jnp.float32).reshape(NBLK, AB, 3, AB)

    def virt_row(single):
        return virt_product(virt_blocks, single.astype(jnp.float32)).astype(jnp.bfloat16).reshape(-1)

    virt_side = lax.map(virt_row, masked)

    def polar_row(single):
        occ_side = occ_product(single.astype(jnp.float32), occ_blocks).astype(jnp.bfloat16).reshape(-1)
        return jnp.dot(virt_side, occ_side, preferred_element_type=jnp.float32)

    return lax.map(polar_row, masked)
```

```python
import functools

import jax
import jax.numpy as jnp
from jax import lax
from jax.experimental import pallas as pl
from jax.experimental.pallas import tpu as pltpu
from jax.sharding import PartitionSpec as P

MESH = pl.DeviceIdType.MESH
AB = 128
PA = 16
W = 3 * AB
NG = 8
GR = AB // NG
NS = 4
PS = PA // NS
F32 = jnp.float32
BF16 = jnp.bfloat16


def rows(g, size):
    return pl.ds(pl.multiple_of(g * size, size), size)


def side(refs, base):
    return jnp.concatenate(
        [jnp.concatenate([ref[base + u] for ref in refs], axis=0) for u in range(GR)], axis=1
    )


def gram(left, right):
    return lax.dot_general(left, right, (((1,), (1,)), ((), ())), preferred_element_type=F32)


def padded(x):
    return jnp.concatenate([x, jnp.zeros((x.shape[0], 128 - x.shape[1]), F32)], axis=1)


def kernel(
    n_ao,
    tensor, pattern, occ, virt, out,
    own_nat, own_row, mate_nat, mate_row, near, far, t_sib, t_own, t_mate, t_nat, mask, occ_rims, occ_wide, virt_t,
    acc_own, acc_mate, acc_near, acc_third, pair_send, pair_recv, sum_a, sum_b,
    in_sem, occ_ss, occ_rs, near_ss, near_rs, mate_ss, mate_rs, far_ss, far_rs, nsib_ss, nsib_rs, fsib_ss, fsib_rs,
    t_ss, t_rs, pair_ss, pair_rs, a_ss, a_rs, b_ss, b_rs,
):
    l, a = lax.axis_index("ao"), lax.axis_index("aux")
    zl, c = lax.div(a, 2), lax.rem(a, 2)
    zh = lax.rem(l, 2)
    flip = (1 - zl) * 2 + c
    up, down = lax.rem(l + 1, n_ao), lax.rem(l + n_ao - 1, n_ao)
    mate = (l, flip)
    cross = (l + 1 - 2 * zh, flip)
    sib = (l, zl * 2 + 1 - c)
    onward = (lax.rem(l + n_ao + 2 - 4 * zh, n_ao), a)
    backward = (lax.rem(l + n_ao - 2 + 4 * zh, n_ao), a)
    gx, gr = lax.div(l, 8), lax.rem(l, 8)
    n_x = n_ao // 8

    def peer_a(d):
        return gx * 8 + lax.rem(gr + d, 8)

    def peer_b(d):
        return lax.rem(gx + d, n_x) * 8 + gr

    def copy(src, dst, ss, rs, to):
        return pltpu.make_async_remote_copy(
            src_ref=src, dst_ref=dst, send_sem=ss, recv_sem=rs, device_id=to, device_id_type=MESH
        )

    def load(g):
        return pltpu.make_async_copy(tensor.at[:, rows(g, GR), :], own_nat.at[:, rows(g, GR), :], in_sem.at[g])

    def send_near(g):
        return copy(own_row.at[rows(g, GR)], near.at[c, rows(g, GR)], near_ss.at[g], near_rs.at[g], cross)

    def send_mate(s):
        return copy(own_nat.at[rows(s, PS)], mate_nat.at[rows(s, PS)], mate_ss.at[s], mate_rs.at[s], mate)

    def send_far(g):
        return copy(near.at[c, rows(g, GR)], far.at[c, rows(g, GR)], far_ss.at[g], far_rs.at[g], onward)

    def near_sib(g, core):
        return copy(near.at[core, rows(g, GR)], near.at[core, rows(g, GR)], nsib_ss.at[g], nsib_rs.at[g], sib)

    def far_sib(g, core):
        return copy(far.at[core, rows(g, GR)], far.at[core, rows(g, GR)], fsib_ss.at[g], fsib_rs.at[g], sib)

    @pl.loop(0, NG)
    def _(g):
        load(g).start()

    barrier = pltpu.get_barrier_semaphore()
    greeted = [mate, sib, (up, flip), (down, flip), onward, backward]
    greeted += [(peer_a(d), a) for d in range(1, 8)] + [(peer_b(d), a) for d in range(1, n_x)]
    for other in greeted:
        pl.semaphore_signal(barrier, inc=1, device_id=other, device_id_type=MESH)

    for p in range(PA):
        for o in range(3):
            kept = pattern[p, o].astype(F32)
            mask[p, :, o * AB : (o + 1) * AB] = jnp.full((GR, AB), kept, F32).astype(BF16)
    for j in range(3):
        virt_t[j] = virt[:, j * AB : (j + 1) * AB].astype(F32).T.astype(BF16)
    occ_wide[...] = jnp.zeros_like(occ_wide)
    occ_wide[AB:, AB:] = occ[...]
    for acc in (acc_own, acc_mate, acc_near, acc_third):
        acc[...] = jnp.zeros_like(acc)

    pl.semaphore_wait(barrier, len(greeted))

    to_up = copy(occ, occ_rims.at[0], occ_ss.at[0], occ_rs.at[0], (up, flip))
    to_down = copy(occ, occ_rims.at[1], occ_ss.at[1], occ_rs.at[1], (down, flip))
    to_up.start()
    to_down.start()

    @pl.loop(0, NG)
    def _(g):
        load(g).wait()
        kept = own_nat[:, rows(g, GR), :] * mask[...]
        own_nat[:, rows(g, GR), :] = kept
        own_row[rows(g, GR)] = jnp.swapaxes(kept, 0, 1)
        send_near(g).start()

    @pl.loop(0, NS)
    def _(s):
        send_mate(s).start()

    to_up.wait_recv()
    to_down.wait_recv()
    occ_wide[:AB, :W] = occ_rims[0]

    def transform(nat, s, offsets):
        x = nat[rows(s, PS)].reshape(PS * AB, W)
        first = jnp.dot(x[:, : 2 * AB], occ_wide[...], preferred_element_type=F32)
        second = jnp.dot(x[:, 2 * AB :], occ_rims[1], preferred_element_type=F32)
        side_occ = jnp.concatenate(
            [first[:, : 2 * AB], first[:, 2 * AB :] + second[:, : 2 * AB], second[:, 2 * AB :]], axis=1
        ).astype(BF16)
        for q in range(PS):
            block = side_occ[q * AB : (q + 1) * AB]
            for j in offsets:
                part = jnp.dot(virt_t[j], block[:, j * AB : j * AB + W], preferred_element_type=F32)
                t_nat[j, s * PS + q] = part.astype(BF16)

    def to_rows(nat, dst, g):
        dst[rows(g, GR)] = jnp.swapaxes(nat[:, rows(g, GR), :], 0, 1)

    def pass_on(g):
        send_near(g).wait_recv()
        send_far(g).start()
        near_sib(g, c).start()

    @pl.loop(0, NS)
    def _(s):
        transform(own_nat, s, (0, 1, 2))

    @pl.loop(0, NG)
    def _(g):
        for j in range(3):
            to_rows(t_nat.at[j], t_own.at[j], g)

    share = copy(t_own.at[1], t_sib, t_ss, t_rs, sib)
    share.start()
    inward, outward = 2 - 2 * zh, 2 * zh
    t_in, t_out = t_own.at[inward], t_own.at[outward]
    m_in, m_out = t_mate.at[inward], t_mate.at[outward]
    near_both = [near.at[0], near.at[1]]
    far_both = [far.at[0], far.at[1]]

    def use_near(g):
        near_sib(g, 1 - c).wait_recv()
        acc_near[...] += gram(side([t_in], g * GR), side(near_both, g * GR))

    def take_far(g):
        send_far(g).wait_recv()
        far_sib(g, c).start()

    def use_far(g):
        far_sib(g, 1 - c).wait_recv()
        acc_near[...] += gram(side([t_out], g * GR), side(far_both, g * GR))

    pass_on(0)
    share.wait_recv()

    @pl.loop(0, NG)
    def _(g):
        @pl.when(g + 1 < NG)
        def _():
            pass_on(g + 1)

        acc_own[...] += gram(side([t_own.at[1], t_sib], g * GR), side([own_row], g * GR))
        use_near(g)

        @pl.when(lax.rem(g, 2) == 1)
        def _():
            s = lax.div(g, 2)
            send_mate(s).wait_recv()
            transform(mate_nat, s, (0, 2))

        @pl.when(g >= 1)
        def _():
            take_far(g - 1)

        @pl.when(g >= 2)
        def _():
            use_far(g - 2)

    @pl.loop(0, NG)
    def _(g):
        for j in (0, 2):
            to_rows(t_nat.at[j], t_mate.at[j], g)
        to_rows(mate_nat, mate_row, g)
        acc_mate[...] += gram(side([t_own.at[1], t_sib], g * GR), side([mate_row], g * GR))

    take_far(NG - 1)
    use_far(NG - 2)

    @pl.loop(0, NG)
    def _(g):
        acc_third[...] += gram(side([m_in], g * GR), side(near_both, g * GR))

    @pl.loop(0, NG)
    def _(g):
        @pl.when(g == NG - 1)
        def _():
            use_far(NG - 1)

        acc_third[...] += gram(side([m_out], g * GR), side(far_both, g * GR))

    pair_send[0] = padded(jnp.concatenate([acc_own[PA:], acc_mate[PA:]], axis=1))
    pair_send[1] = padded(acc_third[...])
    to_sib = copy(pair_send.at[0], pair_recv.at[0], pair_ss.at[0], pair_rs.at[0], sib)
    to_mate = copy(pair_send.at[1], pair_recv.at[1], pair_ss.at[1], pair_rs.at[1], mate)
    to_sib.start()
    to_mate.start()
    to_sib.wait_recv()
    to_mate.wait_recv()

    def by_core(mine, theirs):
        return jnp.where(
            c == 0, jnp.concatenate([mine, theirs], axis=1), jnp.concatenate([theirs, mine], axis=1)
        )

    from_sib, from_mate = pair_recv[0], pair_recv[1]
    same = by_core(acc_own[:PA], from_sib[:, :PA]) + from_mate[:, : 2 * PA]
    other = by_core(acc_mate[:PA], from_sib[:, PA : 2 * PA]) + acc_near[...]
    whole = jnp.where(
        zl == 0, jnp.concatenate([same, other], axis=1), jnp.concatenate([other, same], axis=1)
    )

    def exchange(value, slots, me, count, ss, rs, peer, other_index):
        slots[me] = value
        for d in range(1, count):
            copy(slots.at[me], slots.at[me], ss.at[d], rs.at[me], (peer(d), a)).start()
        for d in range(1, count):
            slot = other_index(d)
            copy(slots.at[slot], slots.at[slot], ss.at[d], rs.at[slot], (peer(d), a)).wait_recv()
        total = slots[0]
        for i in range(1, count):
            total = total + slots[i]
        return total

    part = exchange(padded(whole), sum_a, gr, 8, a_ss, a_rs, peer_a, lambda d: lax.rem(gr + d, 8))
    total = exchange(part, sum_b, gx, n_x, b_ss, b_rs, peer_b, lambda d: lax.rem(gx + d, n_x))
    out[...] = total[:, : 4 * PA]

    to_up.wait_send()
    to_down.wait_send()
    share.wait_send()
    to_sib.wait_send()
    to_mate.wait_send()

    @pl.loop(0, NG)
    def _(g):
        send_near(g).wait_send()
        send_far(g).wait_send()
        near_sib(g, c).wait_send()
        far_sib(g, c).wait_send()

    @pl.loop(0, NS)
    def _(s):
        send_mate(s).wait_send()

    for d in range(1, 8):
        copy(sum_a.at[gr], sum_a.at[gr], a_ss.at[d], a_rs.at[gr], (peer_a(d), a)).wait_send()
    for d in range(1, n_x):
        copy(sum_b.at[gx], sum_b.at[gx], b_ss.at[d], b_rs.at[gx], (peer_b(d), a)).wait_send()


def solution(mesh):
    n_ao = mesh.shape["ao"]
    dma = pltpu.SemaphoreType.DMA
    row = (AB, PA, W)
    nat = (PA, AB, W)
    vmem = pl.BlockSpec(memory_space=pltpu.VMEM)

    def on_device(tensor, pattern, occ, virt):
        return pl.pallas_call(
            functools.partial(kernel, n_ao),
            out_shape=jax.ShapeDtypeStruct((PA, 4 * PA), F32),
            in_specs=[
                pl.BlockSpec(memory_space=pl.ANY),
                pl.BlockSpec(memory_space=pltpu.SMEM),
                vmem,
                vmem,
            ],
            out_specs=vmem,
            scratch_shapes=[
                pltpu.VMEM(nat, BF16),
                pltpu.VMEM(row, BF16),
                pltpu.VMEM(nat, BF16),
                pltpu.VMEM(row, BF16),
                pltpu.VMEM((2, *row), BF16),
                pltpu.VMEM((2, *row), BF16),
                pltpu.VMEM(row, BF16),
                pltpu.VMEM((3, *row), BF16),
                pltpu.VMEM((3, *row), BF16),
                pltpu.VMEM((3, *nat), BF16),
                pltpu.VMEM((PA, GR, W), BF16),
                pltpu.VMEM((2, AB, W), BF16),
                pltpu.VMEM((2 * AB, 4 * AB), BF16),
                pltpu.VMEM((3, AB, AB), BF16),
                pltpu.VMEM((2 * PA, PA), F32),
                pltpu.VMEM((2 * PA, PA), F32),
                pltpu.VMEM((PA, 2 * PA), F32),
                pltpu.VMEM((PA, 2 * PA), F32),
                pltpu.VMEM((2, PA, 128), F32),
                pltpu.VMEM((2, PA, 128), F32),
                pltpu.VMEM((8, PA, 128), F32),
                pltpu.VMEM((n_ao // 8, PA, 128), F32),
                dma((NG,)),
                dma((2,)),
                dma((2,)),
                dma((NG,)),
                dma((NG,)),
                dma((NS,)),
                dma((NS,)),
                dma((NG,)),
                dma((NG,)),
                dma((NG,)),
                dma((NG,)),
                dma((NG,)),
                dma((NG,)),
                dma(()),
                dma(()),
                dma((2,)),
                dma((2,)),
                dma((8,)),
                dma((8,)),
                dma((n_ao // 8,)),
                dma((n_ao // 8,)),
            ],
            compiler_params=pltpu.CompilerParams(
                collective_id=0, has_side_effects=True, vmem_limit_bytes=52 << 20
            ),
        )(tensor, pattern, occ, virt)

    return jax.shard_map(
        on_device,
        mesh=mesh,
        in_specs=(P("aux", "ao", None), P("aux", "ao"), P("ao", None), P("ao", None)),
        out_specs=P("aux", None),
        check_vma=False,
    )
```

```python
import functools

import jax
import jax.numpy as jnp
from jax import lax
from jax.experimental import pallas as pl
from jax.experimental.pallas import tpu as pltpu
from jax.sharding import PartitionSpec as P

MESH = pl.DeviceIdType.MESH
AB = 128
PA = 16
W = 3 * AB
NG = 8
GR = AB // NG
PS = 4
F32 = jnp.float32
BF16 = jnp.bfloat16


def rows(g, size):
    return pl.ds(pl.multiple_of(g * size, size), size)


def side(refs, g, count=GR):
    return jnp.concatenate(
        [jnp.concatenate([ref[g * count + u] for ref in refs], axis=0) for u in range(count)], axis=1
    )


def gram(left, right):
    return lax.dot_general(left, right, (((1,), (1,)), ((), ())), preferred_element_type=F32)


def folded(x):
    return jnp.concatenate([x[:8], x[8:]], axis=1)


def kernel(
    n_ao,
    tensor_hbm, pattern_hbm, occ_hbm, virt_hbm, out,
    pattern, occ, virt,
    own_nat, own_row, mate_row, near, far, t_sib, t_own, t_mate, t_nat, o_mate, mask, occ_rims, occ_wide, virt_t,
    acc_own, acc_mate, acc_near, acc_third, abroad, sum_a, sum_b,
    in_sem, arg_sem, occ_ss, occ_rs, near_ss, near_rs, mate_ss, mate_rs, far_ss, far_rs, nsib_ss, nsib_rs, fsib_ss, fsib_rs,
    t_ss, t_rs, a_ss, a_rs, b_ss, b_rs,
):
    l, a = lax.axis_index("ao"), lax.axis_index("aux")
    zl, c = lax.div(a, 2), lax.rem(a, 2)
    zh = lax.rem(l, 2)
    flip = (1 - zl) * 2 + c
    twin = zl * 2 + 1 - c
    up, down = lax.rem(l + 1, n_ao), lax.rem(l + n_ao - 1, n_ao)
    mate = (l, flip)
    cross = (l + 1 - 2 * zh, flip)
    sib = (l, twin)
    onward = (lax.rem(l + n_ao + 2 - 4 * zh, n_ao), a)
    backward = (lax.rem(l + n_ao - 2 + 4 * zh, n_ao), a)
    n_b = 8
    n_a = n_ao // n_b
    ia, ib = lax.div(l, n_b), lax.rem(l, n_b)

    def peer_a(d):
        return lax.rem(ia + d, n_a) * n_b + ib

    def peer_b(d):
        return ia * n_b + lax.rem(ib + d, n_b)

    def copy(src, dst, ss, rs, to):
        return pltpu.make_async_remote_copy(
            src_ref=src, dst_ref=dst, send_sem=ss, recv_sem=rs, device_id=to, device_id_type=MESH
        )

    def load(g):
        return pltpu.make_async_copy(tensor_hbm.at[:, rows(g, GR), :], own_nat.at[:, rows(g, GR), :], in_sem.at[g])

    def send_near(g):
        return copy(own_row.at[rows(g, GR)], near.at[c, rows(g, GR)], near_ss.at[g], near_rs.at[g], cross)

    def send_mate(g):
        return copy(own_row.at[rows(g, GR)], mate_row.at[rows(g, GR)], mate_ss.at[g], mate_rs.at[g], mate)

    def send_far(g):
        return copy(near.at[c, rows(g, GR)], far.at[c, rows(g, GR)], far_ss.at[g], far_rs.at[g], onward)

    def near_sib(g, core):
        return copy(near.at[core, rows(g, GR)], near.at[core, rows(g, GR)], nsib_ss.at[g], nsib_rs.at[g], sib)

    def far_sib(g, core):
        return copy(far.at[core, rows(g, GR)], far.at[core, rows(g, GR)], fsib_ss.at[g], fsib_rs.at[g], sib)

    barrier = pltpu.get_barrier_semaphore()
    greeted = [mate, sib, (up, flip), (down, flip), onward, backward]
    greeted += [(peer_a(d), other) for d in range(1, n_a) for other in (a, twin, flip)]
    greeted += [(peer_b(d), a) for d in range(1, n_b)]
    for other in greeted:
        pl.semaphore_signal(barrier, inc=1, device_id=other, device_id_type=MESH)

    args = [
        pltpu.make_async_copy(src, dst, arg_sem.at[i])
        for i, (src, dst) in enumerate([(pattern_hbm, pattern), (occ_hbm, occ), (virt_hbm, virt)])
    ]
    for arg in args:
        arg.start()

    @pl.loop(0, NG)
    def _(g):
        load(g).start()

    args[0].wait()
    for p in range(PA):
        for o in range(3):
            kept = pattern[o, p].astype(F32)
            mask[p, :, o * AB : (o + 1) * AB] = jnp.full((GR, AB), kept, F32).astype(BF16)

    @pl.loop(0, NG)
    def _(g):
        load(g).wait()
        kept = own_nat[:, rows(g, GR), :] * mask[...]
        own_nat[:, rows(g, GR), :] = kept
        own_row[rows(g, GR)] = jnp.swapaxes(kept, 0, 1)

    args[1].wait()
    pl.semaphore_wait(barrier, len(greeted))

    to_up = copy(occ, occ_rims.at[0], occ_ss.at[0], occ_rs.at[0], (up, flip))
    to_down = copy(occ, occ_rims.at[1], occ_ss.at[1], occ_rs.at[1], (down, flip))
    to_up.start()
    to_down.start()

    @pl.loop(0, NG)
    def _(g):
        send_near(g).start()
        send_mate(g).start()

    args[2].wait()
    for j in range(3):
        virt_t[j] = virt[:, j * AB : (j + 1) * AB].astype(F32).T.astype(BF16)
    occ_wide[...] = jnp.zeros_like(occ_wide)
    occ_wide[AB:, AB:] = occ[...]
    for acc in (acc_own, acc_mate, acc_near, acc_third):
        acc[...] = jnp.zeros_like(acc)
    to_up.wait_recv()
    to_down.wait_recv()
    occ_wide[:AB, :W] = occ_rims[0]

    def occ_product(x):
        first = jnp.dot(x[:, : 2 * AB], occ_wide[...], preferred_element_type=F32)
        second = jnp.dot(x[:, 2 * AB :], occ_rims[1], preferred_element_type=F32)
        return jnp.concatenate(
            [first[:, : 2 * AB], first[:, 2 * AB :] + second[:, : 2 * AB], second[:, 2 * AB :]], axis=1
        ).astype(BF16)

    def virt_product(block, j, p):
        part = jnp.dot(virt_t[j], block[:, j * AB : j * AB + W], preferred_element_type=F32)
        t_nat[j, p] = part.astype(BF16)

    def to_rows(nat, dst, g):
        dst[rows(g, GR)] = jnp.swapaxes(nat[:, rows(g, GR), :], 0, 1)

    def pass_on(g):
        send_near(g).wait_recv()
        send_far(g).start()
        near_sib(g, c).start()

    @pl.loop(0, PA // PS)
    def _(s):
        product = occ_product(own_nat[rows(s, PS)].reshape(PS * AB, W))
        for q in range(PS):
            for j in range(3):
                virt_product(product[q * AB : (q + 1) * AB], j, s * PS + q)

    pass_on(0)

    @pl.loop(0, NG)
    def _(g):
        for j in range(3):
            to_rows(t_nat.at[j], t_own.at[j], g)

    share = copy(t_own.at[1], t_sib, t_ss, t_rs, sib)
    share.start()
    inward, outward = 2 - 2 * zh, 2 * zh
    t_in, t_out = t_own.at[inward], t_own.at[outward]
    m_in, m_out = t_mate.at[inward], t_mate.at[outward]
    t_pair = [t_own.at[1], t_sib]
    near_both = [near.at[0], near.at[1]]
    far_both = [far.at[0], far.at[1]]

    def take_far(g):
        send_far(g).wait_recv()
        far_sib(g, c).start()

    def use_far(g):
        far_sib(g, 1 - c).wait_recv()
        acc_near[...] += gram(side([t_out], g), side(far_both, g))

    pass_on(1)
    share.wait_recv()

    @pl.loop(0, NG)
    def _(g):
        @pl.when((g >= 1) & (g + 1 < NG))
        def _():
            pass_on(g + 1)

        acc_own[...] += gram(side(t_pair, g), side([own_row], g))
        near_sib(g, 1 - c).wait_recv()
        acc_near[...] += gram(side([t_in], g), side(near_both, g))
        send_mate(g).wait_recv()
        acc_mate[...] += gram(side(t_pair, g), side([mate_row], g))
        product = occ_product(mate_row[rows(g, GR)].reshape(GR * PA, W))
        o_mate[:, rows(g, GR), :] = jnp.swapaxes(product.reshape(GR, PA, 5 * AB), 0, 1)

        @pl.when(g >= 1)
        def _():
            take_far(g - 1)

        @pl.when(g >= 2)
        def _():
            use_far(g - 2)

    @pl.loop(0, PA // PS)
    def _(s):
        for q in range(PS):
            block = o_mate[s * PS + q]
            for j in (0, 2):
                virt_product(block, j, s * PS + q)

    @pl.loop(0, NG)
    def _(g):
        for j in (0, 2):
            to_rows(t_nat.at[j], t_mate.at[j], g)

    take_far(NG - 1)
    use_far(NG - 2)

    @pl.loop(0, NG // 2)
    def _(g):
        acc_third[...] += gram(side([m_in], g, 2 * GR), side(near_both, g, 2 * GR))

    use_far(NG - 1)

    @pl.loop(0, NG // 2)
    def _(g):
        acc_third[...] += gram(side([m_out], g, 2 * GR), side(far_both, g, 2 * GR))

    def pick(first, x, y):
        return jnp.where(first, jnp.concatenate([x, y], axis=1), jnp.concatenate([y, x], axis=1))

    none = jnp.zeros((PA, PA), F32)
    none_pair = jnp.zeros((PA, 2 * PA), F32)
    own_same, own_other = pick(c == 0, acc_own[:PA], none), pick(c == 0, acc_mate[:PA], none) + acc_near[...]
    sib_same, sib_other = pick(c == 0, acc_own[PA:], none), pick(c == 0, acc_mate[PA:], none)
    sum_a[ia] = folded(pick(zl == 0, own_same, own_other))
    abroad[0] = folded(pick(zl == 0, sib_same, sib_other))
    abroad[1] = folded(pick(zl == 0, none_pair, acc_third[...]))

    for d in range(n_a):
        copy(abroad.at[0], sum_a.at[n_a + ia], a_ss, a_rs, (peer_a(d), twin)).start()
        copy(abroad.at[1], sum_a.at[2 * n_a + ia], a_ss, a_rs, (peer_a(d), flip)).start()
        if d > 0:
            copy(sum_a.at[ia], sum_a.at[ia], a_ss, a_rs, (peer_a(d), a)).start()
    some = pl.ds(0, 3 * n_a - 1)
    all_a = copy(sum_a.at[some], sum_a.at[some], a_ss, a_rs, mate)
    all_a.wait_recv()
    part = sum_a[0]
    for i in range(1, 3 * n_a):
        part = part + sum_a[i]
    sum_b[ib] = part
    for d in range(1, n_b):
        copy(sum_b.at[ib], sum_b.at[ib], b_ss, b_rs, (peer_b(d), a)).start()
    some = pl.ds(0, n_b - 1)
    all_b = copy(sum_b.at[some], sum_b.at[some], b_ss, b_rs, (peer_b(1), a))
    all_b.wait_recv()
    total = sum_b[0]
    for i in range(1, n_b):
        total = total + sum_b[i]
    out[: PA // 2] = total[:, : 4 * PA]
    out[PA // 2 :] = total[:, 4 * PA :]

    to_up.wait_send()
    to_down.wait_send()
    share.wait_send()
    all_a.wait_send()
    all_b.wait_send()

    @pl.loop(0, NG)
    def _(g):
        send_near(g).wait_send()
        send_mate(g).wait_send()
        send_far(g).wait_send()
        near_sib(g, c).wait_send()
        far_sib(g, c).wait_send()


def solution(mesh):
    n_ao = mesh.shape["ao"]
    dma = pltpu.SemaphoreType.DMA
    row = (AB, PA, W)
    nat = (PA, AB, W)

    def on_device(tensor, pattern, occ, virt):
        buffers = [
            nat, row, row, (2, *row), (2, *row), row, (3, *row), (3, *row), (3, *nat), (PA, AB, 5 * AB),
            (PA, GR, W), (2, AB, W), (2 * AB, 4 * AB), (3, AB, AB),
        ]
        sums = [
            (2 * PA, PA), (2 * PA, PA), (PA, 2 * PA), (PA, 2 * PA), (2, 8, 128), (3 * n_ao // 8, 8, 128), (8, 8, 128),
        ]
        semaphores = [(NG,), (3,), (2,), (2,)] + [(NG,)] * 10 + [()] * 6
        return pl.pallas_call(
            functools.partial(kernel, n_ao),
            out_shape=jax.ShapeDtypeStruct((PA, 4 * PA), F32),
            in_specs=[pl.BlockSpec(memory_space=pltpu.HBM)] * 4,
            out_specs=pl.BlockSpec(memory_space=pltpu.VMEM),
            scratch_shapes=[
                pltpu.SMEM((3, PA), jnp.int32),
                pltpu.VMEM((AB, W), BF16),
                pltpu.VMEM((AB, W), BF16),
                *[pltpu.VMEM(shape, BF16) for shape in buffers],
                *[pltpu.VMEM(shape, F32) for shape in sums],
                *[dma(shape) for shape in semaphores],
            ],
            compiler_params=pltpu.CompilerParams(
                collective_id=0, has_side_effects=True, vmem_limit_bytes=60 << 20
            ),
        )(tensor, pattern.T, occ, virt)

    return jax.shard_map(
        on_device,
        mesh=mesh,
        in_specs=(P("aux", "ao", None), P("aux", "ao"), P("ao", None), P("ao", None)),
        out_specs=P("aux", None),
        check_vma=False,
    )
```

```python
import functools

import jax
import jax.numpy as jnp
from jax import lax
from jax.experimental import pallas as pl
from jax.experimental.pallas import tpu as pltpu
from jax.sharding import PartitionSpec as P

MESH = pl.DeviceIdType.MESH
AB = 128
PA = 16
W = 3 * AB
NG = 8
GR = AB // NG
NC = 16
CR = AB // NC
LAST = 4
LR = CR // LAST
PS = 4
F32 = jnp.float32
BF16 = jnp.bfloat16


def rows(g, size):
    return pl.ds(pl.multiple_of(g * size, size), size)


def side(refs, g, count=GR):
    return jnp.concatenate(
        [jnp.concatenate([ref[g * count + u] for ref in refs], axis=0) for u in range(count)], axis=1
    )


def gram(left, right):
    return lax.dot_general(left, right, (((1,), (1,)), ((), ())), preferred_element_type=F32)


def folded(x):
    return jnp.concatenate([x[:8], x[8:]], axis=1)


def kernel(
    n_ao,
    tensor_hbm, pattern_hbm, occ_hbm, virt_hbm, out,
    pattern, occ, virt,
    own_nat, own_row, mate_row, near, far, t_sib, t_own, t_mate, t_nat, o_mate, mask, occ_rims, occ_wide, virt_t,
    acc_own, acc_mate, acc_cross, abroad, from_sib, sum_a, sum_b,
    in_sem, arg_sem, occ_ss, occ_rs, near_ss, near_rs, mate_ss, mate_rs, far_ss, far_rs, nsib_ss, nsib_rs, fsib_ss, fsib_rs,
    t_ss, t_rs, s_ss, s_rs, a_ss, a_rs, b_ss, b_rs,
):
    l, a = lax.axis_index("ao"), lax.axis_index("aux")
    zl, c = lax.div(a, 2), lax.rem(a, 2)
    zh = lax.rem(l, 2)
    flip = (1 - zl) * 2 + c
    twin = zl * 2 + 1 - c
    up, down = lax.rem(l + 1, n_ao), lax.rem(l + n_ao - 1, n_ao)
    mate = (l, flip)
    cross = (l + 1 - 2 * zh, flip)
    sib = (l, twin)
    onward = (lax.rem(l + n_ao + 2 - 4 * zh, n_ao), a)
    backward = (lax.rem(l + n_ao - 2 + 4 * zh, n_ao), a)
    n_x, n_y = n_ao // 8, 4
    ix, iy = lax.div(l, 8), lax.rem(lax.div(l, 2), 4)

    def peer(dx, dy):
        return (lax.rem(ix + dx, n_x) * n_y + lax.rem(iy + dy, n_y)) * 2 + zh

    def hops(d):
        return sum(min(step, n - step) for step, n in zip(d, (n_x, n_y)))

    far_first = sorted(((dx, dy) for dx in range(n_x) for dy in range(n_y) if dx + dy), key=hops, reverse=True)

    def copy(src, dst, ss, rs, to):
        return pltpu.make_async_remote_copy(
            src_ref=src, dst_ref=dst, send_sem=ss, recv_sem=rs, device_id=to, device_id_type=MESH
        )

    def load(g):
        return pltpu.make_async_copy(tensor_hbm.at[:, rows(g, GR), :], own_nat.at[:, rows(g, GR), :], in_sem.at[g])

    def piece(k):
        return rows(k, CR) if not isinstance(k, int) or k < NC - 1 else pl.ds((NC - 1) * CR + (k - NC + 1) * LR, LR)

    def send_near(k):
        return copy(own_row.at[piece(k)], near.at[c, piece(k)], near_ss.at[k], near_rs.at[k], cross)

    def send_mate(g):
        return copy(own_row.at[rows(g, GR)], mate_row.at[rows(g, GR)], mate_ss.at[g], mate_rs.at[g], mate)

    def send_far(k):
        return copy(near.at[c, piece(k)], far.at[c, piece(k)], far_ss.at[k], far_rs.at[k], onward)

    def near_sib(k, core):
        return copy(near.at[core, piece(k)], near.at[core, piece(k)], nsib_ss.at[k], nsib_rs.at[k], sib)

    def far_sib(k, core):
        return copy(far.at[core, piece(k)], far.at[core, piece(k)], fsib_ss.at[k], fsib_rs.at[k], sib)

    def rim(to):
        return copy(occ, occ_rims.at[c], occ_ss.at[0], occ_rs.at[0], to)

    def rim_sib(core):
        return copy(occ_rims.at[core], occ_rims.at[core], occ_ss.at[1], occ_rs.at[1], sib)

    barrier = pltpu.get_barrier_semaphore()
    greeted = [mate, sib, (up, flip), (down, flip), onward, backward]
    greeted += [(l + 1 - 2 * zh, a)] + [(peer(dx, dy), a) for dx, dy in far_first]
    for other in greeted:
        pl.semaphore_signal(barrier, inc=1, device_id=other, device_id_type=MESH)

    args = [
        pltpu.make_async_copy(src, dst, arg_sem.at[i])
        for i, (src, dst) in enumerate([(pattern_hbm, pattern), (occ_hbm, occ), (virt_hbm, virt)])
    ]
    for arg in args:
        arg.start()

    @pl.loop(0, NG)
    def _(g):
        load(g).start()

    args[0].wait()
    for p in range(PA):
        for o in range(3):
            kept = pattern[o, p].astype(F32)
            mask[p, :, o * AB : (o + 1) * AB] = jnp.full((GR, AB), kept, F32).astype(BF16)

    @pl.loop(0, NG)
    def _(g):
        load(g).wait()
        kept = own_nat[:, rows(g, GR), :] * mask[...]
        own_nat[:, rows(g, GR), :] = kept
        own_row[rows(g, GR)] = jnp.swapaxes(kept, 0, 1)

    args[1].wait()
    pl.semaphore_wait(barrier, len(greeted))

    rim_to = (lax.rem(l + n_ao + 1 - 2 * c, n_ao), flip)
    rim(rim_to).start()

    @pl.loop(0, NG - 1)
    def _(g):
        send_near(2 * g).start()
        send_near(2 * g + 1).start()
        send_mate(g).start()

    for k in range(NC - 2, NC - 1 + LAST):
        send_near(k).start()
    send_mate(NG - 1).start()

    args[2].wait()
    for j in range(3):
        virt_t[j] = virt[:, j * AB : (j + 1) * AB].astype(F32).T.astype(BF16)
    occ_wide[...] = jnp.zeros_like(occ_wide)
    occ_wide[AB:, AB:] = occ[...]
    for acc in (acc_own, acc_mate, acc_cross):
        acc[...] = jnp.zeros_like(acc)

    def occ_product(x):
        first = jnp.dot(x[:, : 2 * AB], occ_wide[...], preferred_element_type=F32)
        second = jnp.dot(x[:, 2 * AB :], occ_rims[1], preferred_element_type=F32)
        return jnp.concatenate(
            [first[:, : 2 * AB], first[:, 2 * AB :] + second[:, : 2 * AB], second[:, 2 * AB :]], axis=1
        ).astype(BF16)

    def virt_product(block, j, p):
        part = jnp.dot(virt_t[j], block[:, j * AB : j * AB + W], preferred_element_type=F32)
        t_nat[j, p] = part.astype(BF16)

    def to_rows(nat, dst, g):
        dst[rows(g, GR)] = jnp.swapaxes(nat[:, rows(g, GR), :], 0, 1)

    def pass_on(k):
        send_near(k).wait_recv()
        send_far(k).start()
        near_sib(k, c).start()

    def take_far(k):
        send_far(k).wait_recv()
        far_sib(k, c).start()

    inward, outward = 2 - 2 * zh, 2 * zh
    t_pair = [t_own.at[1], t_sib]
    near_both = [near.at[0], near.at[1]]
    far_both = [far.at[0], far.at[1]]
    share = copy(t_own.at[1], t_sib, t_ss, t_rs, sib)
    early = PA // PS

    def own_transform(s):
        product = occ_product(own_nat[rows(s, PS)].reshape(PS * AB, W))
        for q in range(PS):
            for j in range(3):
                virt_product(product[q * AB : (q + 1) * AB], j, s * PS + q)

    def mate_group(g):
        send_mate(g).wait_recv()
        product = occ_product(mate_row[rows(g, GR)].reshape(GR * PA, W))
        o_mate[:, rows(g, GR), :] = jnp.swapaxes(product.reshape(GR, PA, 5 * AB), 0, 1)
        acc_mate[...] += gram(side(t_pair, g), side([mate_row], g))

    @pl.loop(0, NC - 1)
    def _(k):
        pass_on(k)

        @pl.when(k >= 3)
        def _():
            take_far(k - 3)

        @pl.when(k == 0)
        def _():
            rim(rim_to).wait_recv()
            rim_sib(c).start()
            rim_sib(1 - c).wait_recv()
            occ_wide[:AB, :W] = occ_rims[0]

        @pl.when(k < early)
        def _():
            own_transform(k)

        @pl.when((k >= early) & (k < 2 * early))
        def _():
            for g in range(2):
                for j in range(3):
                    to_rows(t_nat.at[j], t_own.at[j], 2 * (k - early) + g)

        @pl.when(k == 2 * early - 1)
        def _():
            share.start()

        @pl.when(k == 2 * early)
        def _():
            share.wait_recv()

        @pl.when(k >= 2 * early)
        def _():
            mate_group(k - 2 * early)

        @pl.when((k >= 2 * early) & (k < 3 * early))
        def _():
            for g in range(2):
                at = 2 * (k - 2 * early) + g
                acc_own[...] += gram(side(t_pair, at), side([own_row], at))

    take_far(NC - 4)
    for k in range(NC - 1, NC - 1 + LAST):
        pass_on(k)
    mate_group(NG - 1)

    def pick(first, x, y):
        return jnp.where(first, jnp.concatenate([x, y], axis=1), jnp.concatenate([y, x], axis=1))

    none = jnp.zeros((PA, PA), F32)
    none_pair = jnp.zeros((PA, 2 * PA), F32)
    sib_same, sib_other = pick(c == 0, acc_own[PA:], none), pick(c == 0, acc_mate[PA:], none)
    abroad[0] = folded(pick(zl == 0, sib_same, sib_other))
    to_sib = copy(abroad.at[0], from_sib, s_ss, s_rs, sib)
    to_sib.start()

    for p in range(PA):
        block = o_mate[p]
        for j in (0, 2):
            virt_product(block, j, p)

    take_far(NC - 3)

    @pl.loop(0, NG)
    def _(g):
        for j in (0, 2):
            to_rows(t_nat.at[j], t_mate.at[j], g)

    def cross_gram(j, both, g, count):
        return gram(side([t_own.at[j], t_mate.at[j]], g, count), side(both, g, count))

    @pl.loop(0, NC - 1)
    def _(k):
        near_sib(k, 1 - c).wait_recv()

    for k in range(NC - 1, NC - 1 + LAST):
        near_sib(k, 1 - c).wait_recv()

    acc_cross[...] = cross_gram(inward, near_both, 0, AB // 2) + cross_gram(inward, near_both, 1, AB // 2)
    for k in range(NC - 2, NC - 1 + LAST):
        take_far(k)

    @pl.loop(0, NC - 4)
    def _(k):
        far_sib(k, 1 - c).wait_recv()

    acc_cross[...] += cross_gram(outward, far_both, 0, AB // 2) + cross_gram(outward, far_both, 2, AB // 4)
    for k in range(NC - 4, NC - 1 + LAST):
        far_sib(k, 1 - c).wait_recv()
    acc_cross[...] += cross_gram(outward, far_both, 3, AB // 4)

    own_same = pick(c == 0, acc_own[:PA], none)
    own_other = pick(c == 0, acc_mate[:PA], none) + acc_cross[:PA]
    abroad[1] = folded(pick(zl == 0, none_pair, acc_cross[PA:]))
    to_sib.wait_recv()
    sum_a[0] = folded(pick(zl == 0, own_same, own_other)) + from_sib[...]

    other_hi = l + 1 - 2 * zh
    copy(sum_a.at[0], sum_a.at[1], a_ss, a_rs, (other_hi, a)).start()
    copy(abroad.at[1], sum_a.at[2], a_ss, a_rs, cross).start()
    copy(abroad.at[1], sum_a.at[3], a_ss, a_rs, mate).start()
    some = pl.ds(0, 3)
    all_a = copy(sum_a.at[some], sum_a.at[some], a_ss, a_rs, mate)
    all_a.wait_recv()
    low, high = jnp.where(zh == 0, sum_a[0], sum_a[1]), jnp.where(zh == 0, sum_a[1], sum_a[0])
    low_third, high_third = jnp.where(zh == 0, sum_a[3], sum_a[2]), jnp.where(zh == 0, sum_a[2], sum_a[3])
    column = lax.div(l, 2)
    sum_b[column] = (low + low_third) + (high + high_third)
    for dx, dy in far_first:
        copy(sum_b.at[column], sum_b.at[column], b_ss, b_rs, (peer(dx, dy), a)).start()
    some = pl.ds(0, n_x * n_y - 1)
    all_b = copy(sum_b.at[some], sum_b.at[some], b_ss, b_rs, (peer(1, 0), a))
    all_b.wait_recv()
    total = sum_b[0]
    for i in range(1, n_x * n_y):
        total = total + sum_b[i]
    out[: PA // 2] = total[:, : 4 * PA]
    out[PA // 2 :] = total[:, 4 * PA :]

    rim(rim_to).wait_send()
    rim_sib(c).wait_send()
    share.wait_send()
    to_sib.wait_send()
    all_a.wait_send()
    all_b.wait_send()

    @pl.loop(0, NG)
    def _(g):
        send_mate(g).wait_send()

    def sent(k):
        send_near(k).wait_send()
        send_far(k).wait_send()
        near_sib(k, c).wait_send()
        far_sib(k, c).wait_send()

    pl.loop(0, NC - 1)(sent)
    for k in range(NC - 1, NC - 1 + LAST):
        sent(k)


def solution(mesh):
    n_ao = mesh.shape["ao"]
    dma = pltpu.SemaphoreType.DMA
    row = (AB, PA, W)
    nat = (PA, AB, W)

    def on_device(tensor, pattern, occ, virt):
        buffers = [
            nat, row, row, (2, *row), (2, *row), row, (3, *row), (3, *row), (3, *nat), (PA, AB, 5 * AB),
            (PA, GR, W), (2, AB, W), (2 * AB, 4 * AB), (3, AB, AB),
        ]
        sums = [
            (2 * PA, PA), (2 * PA, PA), (2 * PA, 2 * PA), (2, 8, 128), (8, 128), (4, 8, 128), (n_ao // 2, 8, 128),
        ]
        n_p = NC - 1 + LAST
        semaphores = [(NG,), (3,), (2,), (2,), (n_p,), (n_p,), (NG,), (NG,)] + [(n_p,)] * 6 + [()] * 8
        return pl.pallas_call(
            functools.partial(kernel, n_ao),
            out_shape=jax.ShapeDtypeStruct((PA, 4 * PA), F32),
            in_specs=[pl.BlockSpec(memory_space=pltpu.HBM)] * 4,
            out_specs=pl.BlockSpec(memory_space=pltpu.VMEM),
            scratch_shapes=[
                pltpu.SMEM((3, PA), jnp.int32),
                pltpu.VMEM((AB, W), BF16),
                pltpu.VMEM((AB, W), BF16),
                *[pltpu.VMEM(shape, BF16) for shape in buffers],
                *[pltpu.VMEM(shape, F32) for shape in sums],
                *[dma(shape) for shape in semaphores],
            ],
            compiler_params=pltpu.CompilerParams(
                collective_id=0, has_side_effects=True, vmem_limit_bytes=60 << 20
            ),
        )(tensor, pattern.T, occ, virt)

    return jax.shard_map(
        on_device,
        mesh=mesh,
        in_specs=(P("aux", "ao", None), P("aux", "ao"), P("ao", None), P("ao", None)),
        out_specs=P("aux", None),
        check_vma=False,
    )
```

```python
import functools

import jax
import jax.numpy as jnp
from jax import lax
from jax.experimental import pallas as pl
from jax.experimental.pallas import tpu as pltpu
from jax.sharding import PartitionSpec as P

MESH = pl.DeviceIdType.MESH
AB = 128
PA = 16
W = 3 * AB
NG = 8
GR = AB // NG
NC = 16
CR = AB // NC
LAST = 4
LR = CR // LAST
PS = 4
F32 = jnp.float32
BF16 = jnp.bfloat16


def rows(g, size):
    return pl.ds(pl.multiple_of(g * size, size), size)


def side(refs, g, count=GR):
    return jnp.concatenate(
        [jnp.concatenate([ref[g * count + u] for ref in refs], axis=0) for u in range(count)], axis=1
    )


def gram(left, right):
    return lax.dot_general(left, right, (((1,), (1,)), ((), ())), preferred_element_type=F32)


def folded(x):
    return jnp.concatenate([x[:8], x[8:]], axis=1)


def kernel(
    n_ao,
    tensor_hbm, pattern_hbm, occ_hbm, virt_hbm, out,
    pattern, occ, virt,
    own_nat, own_row, mate_row, near, far, t_sib, t_own, t_mate, t_nat, o_mate, mask, occ_rims, occ_wide, virt_t,
    acc_own, acc_mate, acc_cross, for_sib, from_sib, third, sums,
    in_sem, arg_sem, rim_ss, rim_rs, near_ss, near_rs, mate_ss, mate_rs, far_ss, far_rs, nsib_ss, nsib_rs, fsib_ss, fsib_rs,
    t_ss, t_rs, s_ss, s_rs, sum_ss, sum_rs, entered,
):
    l, a = lax.axis_index("ao"), lax.axis_index("aux")
    zl, c = lax.div(a, 2), lax.rem(a, 2)
    zh = lax.rem(l, 2)
    flip = (1 - zl) * 2 + c
    twin = zl * 2 + 1 - c
    mate = (l, flip)
    cross = (l + 1 - 2 * zh, flip)
    sib = (l, twin)
    onward = (lax.rem(l + n_ao + 2 - 4 * zh, n_ao), a)
    backward = (lax.rem(l + n_ao - 2 + 4 * zh, n_ao), a)
    n_x, n_y = n_ao // 8, 4
    ix, iy = lax.div(l, 8), lax.rem(lax.div(l, 2), 4)

    def peer(step):
        dx, dy, dz = step[:3]
        return (lax.rem(ix + dx, n_x) * n_y + lax.rem(iy + dy, n_y)) * 2 + lax.rem(zh + dz, 2)

    def hops(step):
        dx, dy, dz, other = step
        return min(dx, n_x - dx) + min(dy, n_y - dy) + (1 if other else 2 * dz)

    steps = [(dx, dy, dz, other) for dx in range(n_x) for dy in range(n_y) for dz in range(2) for other in range(2)]
    far_first = sorted((step for step in steps if sum(step)), key=hops, reverse=True)

    def copy(src, dst, ss, rs, to):
        return pltpu.make_async_remote_copy(
            src_ref=src, dst_ref=dst, send_sem=ss, recv_sem=rs, device_id=to, device_id_type=MESH
        )

    def load(g):
        return pltpu.make_async_copy(tensor_hbm.at[:, rows(g, GR), :], own_nat.at[:, rows(g, GR), :], in_sem.at[g])

    def piece(k):
        return rows(k, CR) if not isinstance(k, int) or k < NC - 1 else pl.ds((NC - 1) * CR + (k - NC + 1) * LR, LR)

    def send_near(k):
        return copy(own_row.at[piece(k)], near.at[c, piece(k)], near_ss.at[k], near_rs.at[k], cross)

    def send_mate(g):
        return copy(own_row.at[rows(g, GR)], mate_row.at[rows(g, GR)], mate_ss.at[g], mate_rs.at[g], mate)

    def send_far(k):
        return copy(near.at[c, piece(k)], far.at[c, piece(k)], far_ss.at[k], far_rs.at[k], onward)

    def near_sib(k, core):
        return copy(near.at[core, piece(k)], near.at[core, piece(k)], nsib_ss.at[k], nsib_rs.at[k], sib)

    def far_sib(k, core):
        return copy(far.at[core, piece(k)], far.at[core, piece(k)], fsib_ss.at[k], fsib_rs.at[k], sib)

    half = rows(c, AB // 2)

    def rim_in():
        return copy(occ.at[half], occ_rims.at[zh, half], rim_ss.at[0], rim_rs.at[0], cross)

    def rim_out():
        return copy(occ_rims.at[1 - zh, half], occ_rims.at[zh, half], rim_ss.at[1], rim_rs.at[1], onward)

    def rim_sib(outer, core):
        at = (zh if outer else 1 - zh), rows(core, AB // 2)
        return copy(occ_rims.at[at], occ_rims.at[at], rim_ss.at[2 + outer], rim_rs.at[2 + outer], sib)

    barrier = pltpu.get_barrier_semaphore()
    def across(bit):
        return l + bit * (1 - 2 * lax.rem(lax.div(l, bit), 2)), a

    halves = [mate] + [across(bit) for bit in (1, 2, 4, 8, 16)]
    greeted = [sib, cross, onward, backward, *halves]
    for other in greeted:
        pl.semaphore_signal(barrier, inc=1, device_id=other, device_id_type=MESH)

    args = [
        pltpu.make_async_copy(src, dst, arg_sem.at[i])
        for i, (src, dst) in enumerate([(pattern_hbm, pattern), (occ_hbm, occ), (virt_hbm, virt)])
    ]
    for arg in args:
        arg.start()

    @pl.loop(0, NG)
    def _(g):
        load(g).start()

    args[0].wait()
    for p in range(PA):
        for o in range(3):
            kept = pattern[o, p].astype(F32)
            mask[p, :, o * AB : (o + 1) * AB] = jnp.full((GR, AB), kept, F32).astype(BF16)

    @pl.loop(0, NG)
    def _(g):
        load(g).wait()
        kept = own_nat[:, rows(g, GR), :] * mask[...]
        own_nat[:, rows(g, GR), :] = kept
        own_row[rows(g, GR)] = jnp.swapaxes(kept, 0, 1)

    args[1].wait()
    pl.semaphore_wait(barrier, len(greeted))

    rim_in().start()

    @pl.loop(0, NG - 1)
    def _(g):
        send_near(2 * g).start()
        send_near(2 * g + 1).start()
        send_mate(g).start()

    for k in range(NC - 2, NC - 1 + LAST):
        send_near(k).start()
    send_mate(NG - 1).start()

    args[2].wait()
    for j in range(3):
        virt_t[j] = virt[:, j * AB : (j + 1) * AB].astype(F32).T.astype(BF16)
    occ_wide[...] = jnp.zeros_like(occ_wide)
    occ_wide[AB:, AB:] = occ[...]
    for acc in (acc_own, acc_mate, acc_cross):
        acc[...] = jnp.zeros_like(acc)

    def occ_product(x):
        first = jnp.dot(x[:, : 2 * AB], occ_wide[...], preferred_element_type=F32)
        second = jnp.dot(x[:, 2 * AB :], occ_rims[1], preferred_element_type=F32)
        return jnp.concatenate(
            [first[:, : 2 * AB], first[:, 2 * AB :] + second[:, : 2 * AB], second[:, 2 * AB :]], axis=1
        ).astype(BF16)

    def virt_product(block, j, p):
        part = jnp.dot(virt_t[j], block[:, j * AB : j * AB + W], preferred_element_type=F32)
        t_nat[j, p] = part.astype(BF16)

    def to_rows(nat, dst, g):
        dst[rows(g, GR)] = jnp.swapaxes(nat[:, rows(g, GR), :], 0, 1)

    def pass_on(k):
        send_near(k).wait_recv()
        send_far(k).start()
        near_sib(k, c).start()

    def take_far(k):
        send_far(k).wait_recv()
        far_sib(k, c).start()

    inward, outward = 2 - 2 * zh, 2 * zh
    t_pair = [t_own.at[1], t_sib]
    near_both = [near.at[0], near.at[1]]
    far_both = [far.at[0], far.at[1]]
    share = copy(t_own.at[1], t_sib, t_ss, t_rs, sib)
    early = PA // PS

    def own_transform(s):
        product = occ_product(own_nat[rows(s, PS)].reshape(PS * AB, W))
        for q in range(PS):
            for j in range(3):
                virt_product(product[q * AB : (q + 1) * AB], j, s * PS + q)

    def own_rows(g):
        for j in range(3):
            to_rows(t_nat.at[j], t_own.at[j], g)

    def mate_group(g):
        send_mate(g).wait_recv()
        product = occ_product(mate_row[rows(g, GR)].reshape(GR * PA, W))
        o_mate[:, rows(g, GR), :] = jnp.swapaxes(product.reshape(GR, PA, 5 * AB), 0, 1)
        acc_mate[...] += gram(side(t_pair, g), side([mate_row], g))

    def own_group(g):
        acc_own[...] += gram(side(t_pair, g), side([own_row], g))

    def at(k, first, last=None):
        return pl.when(k == first if last is None else (k >= first) & (k <= last))

    @pl.loop(0, NC - 1)
    def _(k):
        pass_on(k)

        @pl.when(k >= 3)
        def _():
            take_far(k - 3)
            near_sib(k - 3, 1 - c).wait_recv()

        @pl.when(k >= 6)
        def _():
            far_sib(k - 6, 1 - c).wait_recv()

        for i, other in enumerate(halves):

            @at(k, 2 * i + 1)
            def _(i=i, other=other):
                pl.semaphore_signal(entered.at[i], inc=1, device_id=other, device_id_type=MESH)

            @at(k, 2 * i + 2)
            def _(i=i):
                pl.semaphore_wait(entered.at[i], 1)

        @at(k, 0)
        def _():
            rim_in().wait_recv()
            rim_out().start()
            rim_sib(0, c).start()

        @at(k, 1)
        def _():
            rim_out().wait_recv()
            rim_sib(1, c).start()
            rim_sib(0, 1 - c).wait_recv()
            rim_sib(1, 1 - c).wait_recv()
            occ_wide[:AB, :W] = occ_rims[0]

        @at(k, 2, 5)
        def _():
            own_transform(k - 2)

        @at(k, 6, 8)
        def _():
            own_rows(3 * (k - 6))
            own_rows(3 * (k - 6) + 1)

        @at(k, 6, 7)
        def _():
            own_rows(3 * (k - 6) + 2)

        @at(k, 8)
        def _():
            share.start()

        @at(k, 9)
        def _():
            share.wait_recv()
            mate_group(0)

        @at(k, 9, 14)
        def _():
            mate_group(k - 8)

        @at(k, 10, 13)
        def _():
            own_group(2 * (k - 10))
            own_group(2 * (k - 10) + 1)

    take_far(NC - 4)
    for k in range(NC - 1, NC - 1 + LAST):
        pass_on(k)
    mate_group(NG - 1)

    def pick(first, x, y):
        return jnp.where(first, jnp.concatenate([x, y], axis=1), jnp.concatenate([y, x], axis=1))

    none = jnp.zeros((PA, PA), F32)
    none_pair = jnp.zeros((PA, 2 * PA), F32)
    sib_same, sib_other = pick(c == 0, acc_own[PA:], none), pick(c == 0, acc_mate[PA:], none)
    for_sib[...] = folded(pick(zl == 0, sib_same, sib_other))
    to_sib = copy(for_sib, from_sib, s_ss, s_rs, sib)
    to_sib.start()

    for p in range(PA):
        block = o_mate[p]
        for j in (0, 2):
            virt_product(block, j, p)

    take_far(NC - 3)

    @pl.loop(0, NG)
    def _(g):
        for j in (0, 2):
            to_rows(t_nat.at[j], t_mate.at[j], g)

    def cross_gram(j, both, g, count):
        return gram(side([t_own.at[j], t_mate.at[j]], g, count), side(both, g, count))

    for k in range(NC - 4, NC - 1 + LAST):
        near_sib(k, 1 - c).wait_recv()

    acc_cross[...] = cross_gram(inward, near_both, 0, AB // 2) + cross_gram(inward, near_both, 1, AB // 2)
    for k in range(NC - 2, NC - 1 + LAST):
        take_far(k)
    for k in range(NC - 7, NC - 4):
        far_sib(k, 1 - c).wait_recv()
    acc_cross[...] += cross_gram(outward, far_both, 0, AB // 2) + cross_gram(outward, far_both, 2, AB // 4)
    for k in range(NC - 4, NC - 1 + LAST):
        far_sib(k, 1 - c).wait_recv()
    acc_cross[...] += cross_gram(outward, far_both, 3, AB // 4)

    own_same = pick(c == 0, acc_own[:PA], none)
    own_other = pick(c == 0, acc_mate[:PA], none) + acc_cross[:PA]
    third[...] = folded(pick(zl == 0, none_pair, acc_cross[PA:]))
    to_sib.wait_recv()
    sums[l] = folded(pick(zl == 0, own_same, own_other)) + from_sib[...]

    def piece_to(step):
        src, slot, aux = (third, n_ao + l, flip) if step[3] else (sums.at[l], l, a)
        return copy(src, sums.at[slot], sum_ss, sum_rs, (peer(step), aux))

    for step in far_first:
        piece_to(step).start()

    def sent(k):
        send_near(k).wait_send()
        send_far(k).wait_send()
        near_sib(k, c).wait_send()
        far_sib(k, c).wait_send()

    pl.loop(0, NC - 1)(sent)
    for k in range(NC - 1, NC - 1 + LAST):
        sent(k)

    @pl.loop(0, NG)
    def _(g):
        send_mate(g).wait_send()

    for sent_rim in (rim_in(), rim_out(), rim_sib(0, c), rim_sib(1, c), share, to_sib):
        sent_rim.wait_send()

    most = pl.ds(0, 2 * n_ao - 1)
    everything = copy(sums.at[most], sums.at[most], sum_ss, sum_rs, mate)
    everything.wait_recv()
    total = [sums[i] for i in range(2 * n_ao)]
    while len(total) > 1:
        total = [x + y for x, y in zip(total[::2], total[1::2])]
    out[: PA // 2] = total[0][:, : 4 * PA]
    out[PA // 2 :] = total[0][:, 4 * PA :]
    everything.wait_send()


def solution(mesh):
    n_ao = mesh.shape["ao"]
    dma = pltpu.SemaphoreType.DMA
    row = (AB, PA, W)
    nat = (PA, AB, W)

    def on_device(tensor, pattern, occ, virt):
        buffers = [
            nat, row, row, (2, *row), (2, *row), row, (3, *row), (3, *row), (3, *nat), (PA, AB, 5 * AB),
            (PA, GR, W), (2, AB, W), (2 * AB, 4 * AB), (3, AB, AB),
        ]
        sums = [
            (2 * PA, PA), (2 * PA, PA), (2 * PA, 2 * PA), (8, 128), (8, 128), (8, 128), (2 * n_ao, 8, 128),
        ]
        n_p = NC - 1 + LAST
        semaphores = [(NG,), (3,), (4,), (4,), (n_p,), (n_p,), (NG,), (NG,)] + [(n_p,)] * 6 + [()] * 6
        return pl.pallas_call(
            functools.partial(kernel, n_ao),
            out_shape=jax.ShapeDtypeStruct((PA, 4 * PA), F32),
            in_specs=[pl.BlockSpec(memory_space=pltpu.HBM)] * 4,
            out_specs=pl.BlockSpec(memory_space=pltpu.VMEM),
            scratch_shapes=[
                pltpu.SMEM((3, PA), jnp.int32),
                pltpu.VMEM((AB, W), BF16),
                pltpu.VMEM((AB, W), BF16),
                *[pltpu.VMEM(shape, BF16) for shape in buffers],
                *[pltpu.VMEM(shape, F32) for shape in sums],
                *[dma(shape) for shape in semaphores],
                pltpu.SemaphoreType.REGULAR((6,)),
            ],
            compiler_params=pltpu.CompilerParams(
                collective_id=0, has_side_effects=True, vmem_limit_bytes=60 << 20
            ),
        )(tensor, pattern.T, occ, virt)

    return jax.shard_map(
        on_device,
        mesh=mesh,
        in_specs=(P("aux", "ao", None), P("aux", "ao"), P("ao", None), P("ao", None)),
        out_specs=P("aux", None),
        check_vma=False,
    )
```

```python
import functools

import jax
import jax.numpy as jnp
from jax import lax
from jax.experimental import pallas as pl
from jax.experimental.pallas import tpu as pltpu
from jax.sharding import PartitionSpec as P

MESH = pl.DeviceIdType.MESH
AB = 128
PA = 16
W = 3 * AB
NG = 8
GR = AB // NG
NC = 16
CR = AB // NC
LAST = 4
LR = CR // LAST
PS = 4
F32 = jnp.float32
BF16 = jnp.bfloat16


def rows(g, size):
    return pl.ds(pl.multiple_of(g * size, size), size)


def side(refs, g, count=GR):
    return jnp.concatenate(
        [jnp.concatenate([ref[g * count + u] for ref in refs], axis=0) for u in range(count)], axis=1
    )


def gram(left, right):
    return lax.dot_general(left, right, (((1,), (1,)), ((), ())), preferred_element_type=F32)


def folded(x):
    return jnp.concatenate([x[:8], x[8:]], axis=1)


def kernel(
    n_ao,
    tensor_hbm, pattern_hbm, occ_hbm, virt_hbm, out,
    pattern, occ, virt,
    own_nat, own_row, mate_row, near, far, t_sib, t_own, t_mate, t_nat, o_mate, mask, occ_rims, occ_wide, virt_t,
    acc_own, acc_mate, acc_cross, for_sib, from_sib, third, sums,
    in_sem, arg_sem, rim_ss, rim_rs, near_ss, near_rs, mate_ss, mate_rs, far_ss, far_rs, nsib_ss, nsib_rs, fsib_ss, fsib_rs,
    t_ss, t_rs, s_ss, s_rs, sum_ss, sum_rs, entered,
):
    l, a = lax.axis_index("ao"), lax.axis_index("aux")
    zl, c = lax.div(a, 2), lax.rem(a, 2)
    zh = lax.rem(l, 2)
    flip = (1 - zl) * 2 + c
    twin = zl * 2 + 1 - c
    mate = (l, flip)
    cross = (l + 1 - 2 * zh, flip)
    sib = (l, twin)
    onward = (lax.rem(l + n_ao + 2 - 4 * zh, n_ao), a)
    backward = (lax.rem(l + n_ao - 2 + 4 * zh, n_ao), a)
    n_x, n_y = n_ao // 8, 4
    ix, iy = lax.div(l, 8), lax.rem(lax.div(l, 2), 4)

    def peer(step):
        dx, dy, dz = step[:3]
        return (lax.rem(ix + dx, n_x) * n_y + lax.rem(iy + dy, n_y)) * 2 + lax.rem(zh + dz, 2)

    def hops(step):
        dx, dy, dz, other = step
        return min(dx, n_x - dx) + min(dy, n_y - dy) + (1 if other else 2 * dz)

    steps = [(dx, dy, dz, other) for dx in range(n_x) for dy in range(n_y) for dz in range(2) for other in range(2)]
    far_first = sorted((step for step in steps if sum(step)), key=hops, reverse=True)

    def copy(src, dst, ss, rs, to):
        return pltpu.make_async_remote_copy(
            src_ref=src, dst_ref=dst, send_sem=ss, recv_sem=rs, device_id=to, device_id_type=MESH
        )

    def load(g):
        return pltpu.make_async_copy(tensor_hbm.at[:, rows(g, GR), :], own_nat.at[:, rows(g, GR), :], in_sem.at[g])

    def piece(k):
        return rows(k, CR) if not isinstance(k, int) or k < NC - 1 else pl.ds((NC - 1) * CR + (k - NC + 1) * LR, LR)

    def send_near(k):
        return copy(own_row.at[piece(k)], near.at[c, piece(k)], near_ss.at[k], near_rs.at[k], cross)

    def send_mate(g):
        return copy(own_row.at[rows(g, GR)], mate_row.at[rows(g, GR)], mate_ss.at[g], mate_rs.at[g], mate)

    def send_far(k):
        return copy(near.at[c, piece(k)], far.at[c, piece(k)], far_ss.at[k], far_rs.at[k], onward)

    def near_sib(k, core):
        return copy(near.at[core, piece(k)], near.at[core, piece(k)], nsib_ss.at[k], nsib_rs.at[k], sib)

    def far_sib(k, core):
        return copy(far.at[core, piece(k)], far.at[core, piece(k)], fsib_ss.at[k], fsib_rs.at[k], sib)

    half = rows(c, AB // 2)

    def rim_in():
        return copy(occ.at[half], occ_rims.at[zh, half], rim_ss.at[0], rim_rs.at[0], cross)

    def rim_out():
        return copy(occ_rims.at[1 - zh, half], occ_rims.at[zh, half], rim_ss.at[1], rim_rs.at[1], onward)

    def rim_sib(outer, core):
        at = (zh if outer else 1 - zh), rows(core, AB // 2)
        return copy(occ_rims.at[at], occ_rims.at[at], rim_ss.at[2 + outer], rim_rs.at[2 + outer], sib)

    barrier = pltpu.get_barrier_semaphore()
    def across(bit):
        return l + bit * (1 - 2 * lax.rem(lax.div(l, bit), 2)), a

    halves = [mate] + [across(bit) for bit in (1, 2, 4, 8, 16)]
    greeted = [sib, cross, onward, backward, *halves]
    for other in greeted:
        pl.semaphore_signal(barrier, inc=1, device_id=other, device_id_type=MESH)

    args = [
        pltpu.make_async_copy(src, dst, arg_sem.at[i])
        for i, (src, dst) in enumerate([(pattern_hbm, pattern), (occ_hbm, occ), (virt_hbm, virt)])
    ]
    for arg in args:
        arg.start()

    @pl.loop(0, NG)
    def _(g):
        load(g).start()

    args[0].wait()
    for p in range(PA):
        for o in range(3):
            kept = pattern[o, p].astype(F32)
            mask[p, :, o * AB : (o + 1) * AB] = jnp.full((GR, AB), kept, F32).astype(BF16)

    def mask_group(g):
        load(g).wait()
        kept = own_nat[:, rows(g, GR), :] * mask[...]
        own_nat[:, rows(g, GR), :] = kept
        own_row[rows(g, GR)] = jnp.swapaxes(kept, 0, 1)

    def send_group(g):
        send_near(2 * g).start()

        @pl.when(g < NG - 1)
        def _():
            send_near(2 * g + 1).start()

        @pl.when(g < NG - 1)
        def _():
            send_mate(g).start()

    ahead = 2
    pl.loop(0, ahead)(mask_group)
    args[1].wait()
    pl.semaphore_wait(barrier, len(greeted))
    rim_in().start()

    @pl.loop(0, NG)
    def _(g):
        send_group(g)

        @pl.when(g < NG - ahead)
        def _():
            mask_group(g + ahead)

    for k in range(NC - 1, NC - 1 + LAST):
        send_near(k).start()
    send_mate(NG - 1).start()

    args[2].wait()
    for j in range(3):
        virt_t[j] = virt[:, j * AB : (j + 1) * AB].astype(F32).T.astype(BF16)
    occ_wide[...] = jnp.zeros_like(occ_wide)
    occ_wide[AB:, AB:] = occ[...]
    for acc in (acc_own, acc_mate, acc_cross):
        acc[...] = jnp.zeros_like(acc)

    def occ_product(x):
        first = jnp.dot(x[:, : 2 * AB], occ_wide[...], preferred_element_type=F32)
        second = jnp.dot(x[:, 2 * AB :], occ_rims[1], preferred_element_type=F32)
        return jnp.concatenate(
            [first[:, : 2 * AB], first[:, 2 * AB :] + second[:, : 2 * AB], second[:, 2 * AB :]], axis=1
        ).astype(BF16)

    def virt_product(block, j, p):
        part = jnp.dot(virt_t[j], block[:, j * AB : j * AB + W], preferred_element_type=F32)
        t_nat[j, p] = part.astype(BF16)

    def to_rows(nat, dst, g):
        dst[rows(g, GR)] = jnp.swapaxes(nat[:, rows(g, GR), :], 0, 1)

    def pass_on(k):
        send_near(k).wait_recv()
        send_far(k).start()
        near_sib(k, c).start()

    def take_far(k):
        send_far(k).wait_recv()
        far_sib(k, c).start()

    inward, outward = 2 - 2 * zh, 2 * zh
    t_pair = [t_own.at[1], t_sib]
    near_both = [near.at[0], near.at[1]]
    far_both = [far.at[0], far.at[1]]
    share = copy(t_own.at[1], t_sib, t_ss, t_rs, sib)
    early = PA // PS

    def own_transform(s):
        product = occ_product(own_nat[rows(s, PS)].reshape(PS * AB, W))
        for q in range(PS):
            for j in range(3):
                virt_product(product[q * AB : (q + 1) * AB], j, s * PS + q)

    def own_rows(g):
        for j in range(3):
            to_rows(t_nat.at[j], t_own.at[j], g)

    def mate_group(g):
        send_mate(g).wait_recv()
        product = occ_product(mate_row[rows(g, GR)].reshape(GR * PA, W))
        o_mate[:, rows(g, GR), :] = jnp.swapaxes(product.reshape(GR, PA, 5 * AB), 0, 1)
        acc_mate[...] += gram(side(t_pair, g), side([mate_row], g))

    def own_group(g):
        acc_own[...] += gram(side(t_pair, g), side([own_row], g))

    def at(k, first, last=None):
        return pl.when(k == first if last is None else (k >= first) & (k <= last))

    @pl.loop(0, NC)
    def _(k):
        @pl.when(k < NC - 1)
        def _():
            pass_on(k)

        @pl.when((k >= 3) & (k < NC - 1))
        def _():
            take_far(k - 3)
            near_sib(k - 3, 1 - c).wait_recv()

        @pl.when((k >= 6) & (k < NC - 1))
        def _():
            far_sib(k - 6, 1 - c).wait_recv()

        @at(k, NC - 1)
        def _():
            take_far(NC - 4)
            for last in range(NC - 1, NC - 1 + LAST):
                pass_on(last)

        for i, other in enumerate(halves):

            @at(k, 2 * i + 1)
            def _(i=i, other=other):
                pl.semaphore_signal(entered.at[i], inc=1, device_id=other, device_id_type=MESH)

            @at(k, 2 * i + 2)
            def _(i=i):
                pl.semaphore_wait(entered.at[i], 1)

        @at(k, 0)
        def _():
            rim_in().wait_recv()
            rim_out().start()
            rim_sib(0, c).start()

        @at(k, 1)
        def _():
            rim_out().wait_recv()
            rim_sib(1, c).start()
            rim_sib(0, 1 - c).wait_recv()
            rim_sib(1, 1 - c).wait_recv()
            occ_wide[:AB, :W] = occ_rims[0]

        @at(k, 2, 5)
        def _():
            own_transform(k - 2)

        @at(k, 6, 8)
        def _():
            pl.loop(3 * (k - 6), jnp.minimum(3 * (k - 6) + 3, NG))(own_rows)

        @at(k, 8)
        def _():
            share.start()

        @at(k, 9)
        def _():
            share.wait_recv()

        @at(k, 9, NC - 1)
        def _():
            pl.loop(jnp.where(k == 9, 0, k - 8), k - 7)(mate_group)

        @at(k, 10, 13)
        def _():
            pl.loop(2 * (k - 10), 2 * (k - 10) + 2)(own_group)

    def pick(first, x, y):
        return jnp.where(first, jnp.concatenate([x, y], axis=1), jnp.concatenate([y, x], axis=1))

    none = jnp.zeros((PA, PA), F32)
    none_pair = jnp.zeros((PA, 2 * PA), F32)
    sib_same, sib_other = pick(c == 0, acc_own[PA:], none), pick(c == 0, acc_mate[PA:], none)
    for_sib[...] = folded(pick(zl == 0, sib_same, sib_other))
    to_sib = copy(for_sib, from_sib, s_ss, s_rs, sib)
    to_sib.start()

    @pl.loop(0, PA // 8)
    def _(s):
        for q in range(8):
            block = o_mate[8 * s + q]
            for j in (0, 2):
                virt_product(block, j, 8 * s + q)

    take_far(NC - 3)

    @pl.loop(0, NG)
    def _(g):
        for j in (0, 2):
            to_rows(t_nat.at[j], t_mate.at[j], g)

    def cross_gram(j, both, g, count):
        return gram(side([t_own.at[j], t_mate.at[j]], g, count), side(both, g, count))

    for k in range(NC - 4, NC - 1 + LAST):
        near_sib(k, 1 - c).wait_recv()

    @pl.loop(0, 2)
    def _(g):
        acc_cross[...] += cross_gram(inward, near_both, g, AB // 2)

    for k in range(NC - 2, NC - 1 + LAST):
        take_far(k)
    for k in range(NC - 7, NC - 4):
        far_sib(k, 1 - c).wait_recv()
    acc_cross[...] += cross_gram(outward, far_both, 0, AB // 2) + cross_gram(outward, far_both, 2, AB // 4)
    for k in range(NC - 4, NC - 1 + LAST):
        far_sib(k, 1 - c).wait_recv()
    acc_cross[...] += cross_gram(outward, far_both, 3, AB // 4)

    own_same = pick(c == 0, acc_own[:PA], none)
    own_other = pick(c == 0, acc_mate[:PA], none) + acc_cross[:PA]
    third[...] = folded(pick(zl == 0, none_pair, acc_cross[PA:]))
    to_sib.wait_recv()
    sums[l] = folded(pick(zl == 0, own_same, own_other)) + from_sib[...]

    def piece_to(step):
        src, slot, aux = (third, n_ao + l, flip) if step[3] else (sums.at[l], l, a)
        return copy(src, sums.at[slot], sum_ss, sum_rs, (peer(step), aux))

    for step in far_first:
        piece_to(step).start()

    def sent(k):
        send_near(k).wait_send()
        send_far(k).wait_send()
        near_sib(k, c).wait_send()
        far_sib(k, c).wait_send()

    pl.loop(0, NC - 1)(sent)
    for k in range(NC - 1, NC - 1 + LAST):
        sent(k)

    @pl.loop(0, NG)
    def _(g):
        send_mate(g).wait_send()

    for sent_rim in (rim_in(), rim_out(), rim_sib(0, c), rim_sib(1, c), share, to_sib):
        sent_rim.wait_send()

    most = pl.ds(0, 2 * n_ao - 1)
    everything = copy(sums.at[most], sums.at[most], sum_ss, sum_rs, mate)
    everything.wait_recv()
    total = [sums[i] for i in range(2 * n_ao)]
    while len(total) > 1:
        total = [x + y for x, y in zip(total[::2], total[1::2])]
    out[: PA // 2] = total[0][:, : 4 * PA]
    out[PA // 2 :] = total[0][:, 4 * PA :]
    everything.wait_send()


def solution(mesh):
    n_ao = mesh.shape["ao"]
    dma = pltpu.SemaphoreType.DMA
    row = (AB, PA, W)
    nat = (PA, AB, W)

    def on_device(tensor, pattern, occ, virt):
        buffers = [
            nat, row, row, (2, *row), (2, *row), row, (3, *row), (3, *row), (3, *nat), (PA, AB, 5 * AB),
            (PA, GR, W), (2, AB, W), (2 * AB, 4 * AB), (3, AB, AB),
        ]
        sums = [
            (2 * PA, PA), (2 * PA, PA), (2 * PA, 2 * PA), (8, 128), (8, 128), (8, 128), (2 * n_ao, 8, 128),
        ]
        n_p = NC - 1 + LAST
        semaphores = [(NG,), (3,), (4,), (4,), (n_p,), (n_p,), (NG,), (NG,)] + [(n_p,)] * 6 + [()] * 6
        return pl.pallas_call(
            functools.partial(kernel, n_ao),
            out_shape=jax.ShapeDtypeStruct((PA, 4 * PA), F32),
            in_specs=[pl.BlockSpec(memory_space=pltpu.HBM)] * 4,
            out_specs=pl.BlockSpec(memory_space=pltpu.VMEM),
            scratch_shapes=[
                pltpu.SMEM((3, PA), jnp.int32),
                pltpu.VMEM((AB, W), BF16),
                pltpu.VMEM((AB, W), BF16),
                *[pltpu.VMEM(shape, BF16) for shape in buffers],
                *[pltpu.VMEM(shape, F32) for shape in sums],
                *[dma(shape) for shape in semaphores],
                pltpu.SemaphoreType.REGULAR((6,)),
            ],
            compiler_params=pltpu.CompilerParams(
                collective_id=0, has_side_effects=True, vmem_limit_bytes=55200 << 10
            ),
        )(tensor, pattern.T, occ, virt)

    return jax.shard_map(
        on_device,
        mesh=mesh,
        in_specs=(P("aux", "ao", None), P("aux", "ao"), P("ao", None), P("ao", None)),
        out_specs=P("aux", None),
        check_vma=False,
    )
```

```python
import functools

import jax
import jax.numpy as jnp
from jax import lax
from jax.experimental import pallas as pl
from jax.experimental.pallas import tpu as pltpu
from jax.sharding import PartitionSpec as P

MESH = pl.DeviceIdType.MESH
AB = 128
PA = 16
W = 3 * AB
NG = 8
GR = AB // NG
NC = 16
CR = AB // NC
LAST = 4
LR = CR // LAST
PS = 4
F32 = jnp.float32
BF16 = jnp.bfloat16


def rows(g, size):
    return pl.ds(pl.multiple_of(g * size, size), size)


def side(refs, g, count=GR):
    return jnp.concatenate(
        [jnp.concatenate([ref[g * count + u] for ref in refs], axis=0) for u in range(count)], axis=1
    )


def gram(left, right):
    return lax.dot_general(left, right, (((1,), (1,)), ((), ())), preferred_element_type=F32)


def folded(x):
    return jnp.concatenate([x[:8], x[8:]], axis=1)


def kernel(
    n_ao,
    tensor_hbm, pattern_hbm, occ_hbm, virt_hbm, out,
    pattern, occ, virt,
    own_nat, own_row, mate_row, near, far, t_sib, t_own, t_mate, t_nat, o_mate, mask, occ_rims, occ_wide, virt_t,
    acc_own, acc_mate, acc_cross, for_sib, from_sib, third, sums,
    in_sem, arg_sem, rim_ss, rim_rs, near_ss, near_rs, mate_ss, mate_rs, far_ss, far_rs, nsib_ss, nsib_rs, fsib_ss, fsib_rs,
    t_ss, t_rs, s_ss, s_rs, sum_ss, sum_rs, entered,
):
    l, a = lax.axis_index("ao"), lax.axis_index("aux")
    zl, c = lax.div(a, 2), lax.rem(a, 2)
    zh = lax.rem(l, 2)
    flip = (1 - zl) * 2 + c
    twin = zl * 2 + 1 - c
    mate = (l, flip)
    cross = (l + 1 - 2 * zh, flip)
    sib = (l, twin)
    onward = (lax.rem(l + n_ao + 2 - 4 * zh, n_ao), a)
    backward = (lax.rem(l + n_ao - 2 + 4 * zh, n_ao), a)
    n_x, n_y = n_ao // 8, 4
    ix, iy = lax.div(l, 8), lax.rem(lax.div(l, 2), 4)

    def peer(step):
        dx, dy, dz = step[:3]
        return (lax.rem(ix + dx, n_x) * n_y + lax.rem(iy + dy, n_y)) * 2 + lax.rem(zh + dz, 2)

    def hops(step):
        dx, dy, dz, other = step
        return min(dx, n_x - dx) + min(dy, n_y - dy) + (1 if other else 2 * dz)

    steps = [(dx, dy, dz, other) for dx in range(n_x) for dy in range(n_y) for dz in range(2) for other in range(2)]
    far_first = sorted((step for step in steps if sum(step)), key=hops, reverse=True)

    def copy(src, dst, ss, rs, to):
        return pltpu.make_async_remote_copy(
            src_ref=src, dst_ref=dst, send_sem=ss, recv_sem=rs, device_id=to, device_id_type=MESH
        )

    def load(g):
        return pltpu.make_async_copy(tensor_hbm.at[:, rows(g, GR), :], own_nat.at[:, rows(g, GR), :], in_sem.at[g])

    def piece(k):
        return rows(k, CR) if not isinstance(k, int) or k < NC - 1 else pl.ds((NC - 1) * CR + (k - NC + 1) * LR, LR)

    def send_near(k):
        return copy(own_row.at[piece(k)], near.at[c, piece(k)], near_ss.at[k], near_rs.at[k], cross)

    def send_mate(g):
        return copy(own_row.at[rows(g, GR)], mate_row.at[rows(g, GR)], mate_ss.at[g], mate_rs.at[g], mate)

    def send_far(k):
        return copy(near.at[c, piece(k)], far.at[c, piece(k)], far_ss.at[k], far_rs.at[k], onward)

    def near_sib(k, core):
        return copy(near.at[core, piece(k)], near.at[core, piece(k)], nsib_ss.at[k], nsib_rs.at[k], sib)

    def far_sib(k, core):
        return copy(far.at[core, piece(k)], far.at[core, piece(k)], fsib_ss.at[k], fsib_rs.at[k], sib)

    half = rows(c, AB // 2)

    def rim_in():
        return copy(occ.at[half], occ_rims.at[zh, half], rim_ss.at[0], rim_rs.at[0], cross)

    def rim_out():
        return copy(occ_rims.at[1 - zh, half], occ_rims.at[zh, half], rim_ss.at[1], rim_rs.at[1], onward)

    def rim_sib(outer, core):
        at = (zh if outer else 1 - zh), rows(core, AB // 2)
        return copy(occ_rims.at[at], occ_rims.at[at], rim_ss.at[2 + outer], rim_rs.at[2 + outer], sib)

    barrier = pltpu.get_barrier_semaphore()
    def across(bit):
        return l + bit * (1 - 2 * lax.rem(lax.div(l, bit), 2)), a

    halves = [mate] + [across(bit) for bit in (1, 2, 4, 8, 16)]
    greeted = [sib, cross, onward, backward, *halves]
    for other in greeted:
        pl.semaphore_signal(barrier, inc=1, device_id=other, device_id_type=MESH)

    args = [
        pltpu.make_async_copy(src, dst, arg_sem.at[i])
        for i, (src, dst) in enumerate([(pattern_hbm, pattern), (occ_hbm, occ), (virt_hbm, virt)])
    ]
    for arg in args:
        arg.start()

    @pl.loop(0, NG)
    def _(g):
        load(g).start()

    args[0].wait()
    for p in range(PA):
        for o in range(3):
            kept = pattern[o, p].astype(F32)
            mask[p, :, o * AB : (o + 1) * AB] = jnp.full((GR, AB), kept, F32).astype(BF16)

    def mask_group(g):
        load(g).wait()
        kept = own_nat[:, rows(g, GR), :] * mask[...]
        own_nat[:, rows(g, GR), :] = kept
        own_row[rows(g, GR)] = jnp.swapaxes(kept, 0, 1)

    def send_group(g):
        send_near(2 * g).start()

        @pl.when(g < NG - 1)
        def _():
            send_near(2 * g + 1).start()

        @pl.when(g > 0)
        def _():
            send_mate(g - 1).start()

    ahead = 2
    pl.loop(0, ahead)(mask_group)
    args[1].wait()
    pl.semaphore_wait(barrier, len(greeted))
    rim_in().start()

    @pl.loop(0, NG)
    def _(g):
        send_group(g)

        @pl.when(g < NG - ahead)
        def _():
            mask_group(g + ahead)

    for k in range(NC - 1, NC - 1 + LAST):
        send_near(k).start()
    send_mate(NG - 1).start()

    args[2].wait()
    for j in range(3):
        virt_t[j] = virt[:, j * AB : (j + 1) * AB].astype(F32).T.astype(BF16)
    occ_wide[...] = jnp.zeros_like(occ_wide)
    occ_wide[AB:, AB:] = occ[...]
    for acc in (acc_own, acc_mate, acc_cross):
        acc[...] = jnp.zeros_like(acc)

    def occ_product(x):
        first = jnp.dot(x[:, : 2 * AB], occ_wide[...], preferred_element_type=F32)
        second = jnp.dot(x[:, 2 * AB :], occ_rims[1], preferred_element_type=F32)
        return jnp.concatenate(
            [first[:, : 2 * AB], first[:, 2 * AB :] + second[:, : 2 * AB], second[:, 2 * AB :]], axis=1
        ).astype(BF16)

    def virt_product(block, j, p):
        part = jnp.dot(virt_t[j], block[:, j * AB : j * AB + W], preferred_element_type=F32)
        t_nat[j, p] = part.astype(BF16)

    def to_rows(nat, dst, g):
        dst[rows(g, GR)] = jnp.swapaxes(nat[:, rows(g, GR), :], 0, 1)

    def pass_on(k):
        send_near(k).wait_recv()
        send_far(k).start()
        near_sib(k, c).start()

    def take_far(k):
        send_far(k).wait_recv()
        far_sib(k, c).start()

    inward, outward = 2 - 2 * zh, 2 * zh
    t_pair = [t_own.at[1], t_sib]
    near_both = [near.at[0], near.at[1]]
    far_both = [far.at[0], far.at[1]]
    share = copy(t_own.at[1], t_sib, t_ss, t_rs, sib)
    early = PA // PS

    def own_transform(s):
        product = occ_product(own_nat[rows(s, PS)].reshape(PS * AB, W))
        for q in range(PS):
            for j in range(3):
                virt_product(product[q * AB : (q + 1) * AB], j, s * PS + q)

    def own_rows(g):
        for j in range(3):
            to_rows(t_nat.at[j], t_own.at[j], g)

    def mate_group(g):
        send_mate(g).wait_recv()
        product = occ_product(mate_row[rows(g, GR)].reshape(GR * PA, W))
        o_mate[:, rows(g, GR), :] = jnp.swapaxes(product.reshape(GR, PA, 5 * AB), 0, 1)
        acc_mate[...] += gram(side(t_pair, g), side([mate_row], g))

    def own_group(g):
        acc_own[...] += gram(side(t_pair, g), side([own_row], g))

    def at(k, first, last=None):
        return pl.when(k == first if last is None else (k >= first) & (k <= last))

    @pl.loop(0, NC)
    def _(k):
        @pl.when(k < NC - 1)
        def _():
            pass_on(k)

        @pl.when((k >= 3) & (k < NC - 1))
        def _():
            take_far(k - 3)
            near_sib(k - 3, 1 - c).wait_recv()

        @pl.when((k >= 6) & (k < NC - 1))
        def _():
            far_sib(k - 6, 1 - c).wait_recv()

        @at(k, NC - 1)
        def _():
            take_far(NC - 4)
            for last in range(NC - 1, NC - 1 + LAST):
                pass_on(last)

        for i, other in enumerate(halves):

            @at(k, 2 * i + 1)
            def _(i=i, other=other):
                pl.semaphore_signal(entered.at[i], inc=1, device_id=other, device_id_type=MESH)

            @at(k, 2 * i + 2)
            def _(i=i):
                pl.semaphore_wait(entered.at[i], 1)

        @at(k, 0)
        def _():
            rim_in().wait_recv()
            rim_out().start()
            rim_sib(0, c).start()

        @at(k, 1)
        def _():
            rim_out().wait_recv()
            rim_sib(1, c).start()
            rim_sib(0, 1 - c).wait_recv()
            rim_sib(1, 1 - c).wait_recv()
            occ_wide[:AB, :W] = occ_rims[0]

        @at(k, 2, 5)
        def _():
            own_transform(k - 2)

        @at(k, 6, 8)
        def _():
            pl.loop(3 * (k - 6), jnp.minimum(3 * (k - 6) + 3, NG))(own_rows)

        @at(k, 8)
        def _():
            share.start()

        @at(k, 9)
        def _():
            share.wait_recv()

        @at(k, 9, NC - 1)
        def _():
            pl.loop(jnp.where(k == 9, 0, k - 8), k - 7)(mate_group)

        @at(k, 10, 13)
        def _():
            pl.loop(2 * (k - 10), 2 * (k - 10) + 2)(own_group)

    def pick(first, x, y):
        return jnp.where(first, jnp.concatenate([x, y], axis=1), jnp.concatenate([y, x], axis=1))

    none = jnp.zeros((PA, PA), F32)
    none_pair = jnp.zeros((PA, 2 * PA), F32)
    sib_same, sib_other = pick(c == 0, acc_own[PA:], none), pick(c == 0, acc_mate[PA:], none)
    for_sib[...] = folded(pick(zl == 0, sib_same, sib_other))
    to_sib = copy(for_sib, from_sib, s_ss, s_rs, sib)
    to_sib.start()

    @pl.loop(0, PA // 8)
    def _(s):
        for q in range(8):
            block = o_mate[8 * s + q]
            for j in (0, 2):
                virt_product(block, j, 8 * s + q)

    take_far(NC - 3)

    @pl.loop(0, NG)
    def _(g):
        for j in (0, 2):
            to_rows(t_nat.at[j], t_mate.at[j], g)

    def cross_gram(j, both, g, count):
        return gram(side([t_own.at[j], t_mate.at[j]], g, count), side(both, g, count))

    for k in range(NC - 4, NC - 1 + LAST):
        near_sib(k, 1 - c).wait_recv()

    @pl.loop(0, 2)
    def _(g):
        acc_cross[...] += cross_gram(inward, near_both, g, AB // 2)

        @pl.when(g == 0)
        def _():
            take_far(NC - 2)

    for k in range(NC - 1, NC - 1 + LAST):
        take_far(k)
    for k in range(NC - 7, NC - 4):
        far_sib(k, 1 - c).wait_recv()
    acc_cross[...] += cross_gram(outward, far_both, 0, AB // 2) + cross_gram(outward, far_both, 2, AB // 4)
    for k in range(NC - 4, NC - 1 + LAST):
        far_sib(k, 1 - c).wait_recv()
    acc_cross[...] += cross_gram(outward, far_both, 3, AB // 4)

    own_same = pick(c == 0, acc_own[:PA], none)
    own_other = pick(c == 0, acc_mate[:PA], none) + acc_cross[:PA]
    third[...] = folded(pick(zl == 0, none_pair, acc_cross[PA:]))
    to_sib.wait_recv()
    sums[l] = folded(pick(zl == 0, own_same, own_other)) + from_sib[...]

    def piece_to(step):
        src, slot, aux = (third, n_ao + l, flip) if step[3] else (sums.at[l], l, a)
        return copy(src, sums.at[slot], sum_ss, sum_rs, (peer(step), aux))

    for step in far_first:
        piece_to(step).start()

    def sent(k):
        send_near(k).wait_send()
        send_far(k).wait_send()
        near_sib(k, c).wait_send()
        far_sib(k, c).wait_send()

    pl.loop(0, NC - 1)(sent)
    for k in range(NC - 1, NC - 1 + LAST):
        sent(k)

    @pl.loop(0, NG)
    def _(g):
        send_mate(g).wait_send()

    for sent_rim in (rim_in(), rim_out(), rim_sib(0, c), rim_sib(1, c), share, to_sib):
        sent_rim.wait_send()

    most = pl.ds(0, 2 * n_ao - 1)
    everything = copy(sums.at[most], sums.at[most], sum_ss, sum_rs, mate)
    everything.wait_recv()
    total = [sums[i] for i in range(2 * n_ao)]
    while len(total) > 1:
        total = [x + y for x, y in zip(total[::2], total[1::2])]
    out[: PA // 2] = total[0][:, : 4 * PA]
    out[PA // 2 :] = total[0][:, 4 * PA :]
    everything.wait_send()


def solution(mesh):
    n_ao = mesh.shape["ao"]
    dma = pltpu.SemaphoreType.DMA
    row = (AB, PA, W)
    nat = (PA, AB, W)

    def on_device(tensor, pattern, occ, virt):
        buffers = [
            nat, row, row, (2, *row), (2, *row), row, (3, *row), (3, *row), (3, *nat), (PA, AB, 5 * AB),
            (PA, GR, W), (2, AB, W), (2 * AB, 4 * AB), (3, AB, AB),
        ]
        sums = [
            (2 * PA, PA), (2 * PA, PA), (2 * PA, 2 * PA), (8, 128), (8, 128), (8, 128), (2 * n_ao, 8, 128),
        ]
        n_p = NC - 1 + LAST
        semaphores = [(NG,), (3,), (4,), (4,), (n_p,), (n_p,), (NG,), (NG,)] + [(n_p,)] * 6 + [()] * 6
        return pl.pallas_call(
            functools.partial(kernel, n_ao),
            out_shape=jax.ShapeDtypeStruct((PA, 4 * PA), F32),
            in_specs=[pl.BlockSpec(memory_space=pltpu.HBM)] * 4,
            out_specs=pl.BlockSpec(memory_space=pltpu.VMEM),
            scratch_shapes=[
                pltpu.SMEM((3, PA), jnp.int32),
                pltpu.VMEM((AB, W), BF16),
                pltpu.VMEM((AB, W), BF16),
                *[pltpu.VMEM(shape, BF16) for shape in buffers],
                *[pltpu.VMEM(shape, F32) for shape in sums],
                *[dma(shape) for shape in semaphores],
                pltpu.SemaphoreType.REGULAR((6,)),
            ],
            compiler_params=pltpu.CompilerParams(
                collective_id=0, has_side_effects=True, vmem_limit_bytes=55200 << 10
            ),
        )(tensor, pattern.T, occ, virt)

    return jax.shard_map(
        on_device,
        mesh=mesh,
        in_specs=(P("aux", "ao", None), P("aux", "ao"), P("ao", None), P("ao", None)),
        out_specs=P("aux", None),
        check_vma=False,
    )
```

```python
import functools

import jax
import jax.numpy as jnp
from jax import lax
from jax.experimental import pallas as pl
from jax.experimental.pallas import tpu as pltpu
from jax.sharding import PartitionSpec as P

MESH = pl.DeviceIdType.MESH
AB = 128
PA = 16
W = 3 * AB
NG = 8
GR = AB // NG
NC = 16
CR = AB // NC
LAST = 4
LR = CR // LAST
PS = 4
F32 = jnp.float32
BF16 = jnp.bfloat16


def rows(g, size):
    return pl.ds(pl.multiple_of(g * size, size), size)


def side(refs, g, count=GR):
    return jnp.concatenate(
        [jnp.concatenate([ref[g * count + u] for ref in refs], axis=0) for u in range(count)], axis=1
    )


def gram(left, right):
    return lax.dot_general(left, right, (((1,), (1,)), ((), ())), preferred_element_type=F32)


def folded(x):
    return jnp.concatenate([x[:8], x[8:]], axis=1)


def kernel(
    n_ao,
    tensor_hbm, pattern_hbm, occ_hbm, virt_hbm, out,
    pattern, occ, virt,
    own_nat, own_row, mate_row, near, far, t_sib, t_own, t_mate, t_nat, o_mate, mask, occ_rims, occ_wide, virt_t,
    acc_own, acc_mate, acc_cross, for_sib, from_sib, third, sums,
    in_sem, arg_sem, rim_ss, rim_rs, near_ss, near_rs, mate_ss, mate_rs, far_ss, far_rs, nsib_ss, nsib_rs, fsib_ss, fsib_rs,
    t_ss, t_rs, s_ss, s_rs, sum_ss, sum_rs, entered,
):
    l, a = lax.axis_index("ao"), lax.axis_index("aux")
    zl, c = lax.div(a, 2), lax.rem(a, 2)
    zh = lax.rem(l, 2)
    flip = (1 - zl) * 2 + c
    twin = zl * 2 + 1 - c
    mate = (l, flip)
    cross = (l + 1 - 2 * zh, flip)
    sib = (l, twin)
    onward = (lax.rem(l + n_ao + 2 - 4 * zh, n_ao), a)
    backward = (lax.rem(l + n_ao - 2 + 4 * zh, n_ao), a)
    n_x, n_y = n_ao // 8, 4
    ix, iy = lax.div(l, 8), lax.rem(lax.div(l, 2), 4)

    def peer(step):
        dx, dy, dz = step[:3]
        return (lax.rem(ix + dx, n_x) * n_y + lax.rem(iy + dy, n_y)) * 2 + lax.rem(zh + dz, 2)

    def hops(step):
        dx, dy, dz, other = step
        return min(dx, n_x - dx) + min(dy, n_y - dy) + (1 if other else 2 * dz)

    steps = [(dx, dy, dz, other) for dx in range(n_x) for dy in range(n_y) for dz in range(2) for other in range(2)]
    far_first = sorted((step for step in steps if sum(step)), key=lambda step: (hops(step), step[3]), reverse=True)

    def copy(src, dst, ss, rs, to):
        return pltpu.make_async_remote_copy(
            src_ref=src, dst_ref=dst, send_sem=ss, recv_sem=rs, device_id=to, device_id_type=MESH
        )

    def load(g):
        return pltpu.make_async_copy(tensor_hbm.at[:, rows(g, GR), :], own_nat.at[:, rows(g, GR), :], in_sem.at[g])

    def piece(k):
        return rows(k, CR) if not isinstance(k, int) or k < NC - 1 else pl.ds((NC - 1) * CR + (k - NC + 1) * LR, LR)

    def send_near(k):
        return copy(own_row.at[piece(k)], near.at[c, piece(k)], near_ss.at[k], near_rs.at[k], cross)

    def send_mate(g):
        return copy(own_row.at[rows(g, GR)], mate_row.at[rows(g, GR)], mate_ss.at[g], mate_rs.at[g], mate)

    def send_far(k):
        return copy(near.at[c, piece(k)], far.at[c, piece(k)], far_ss.at[k], far_rs.at[k], onward)

    def near_sib(k, core):
        return copy(near.at[core, piece(k)], near.at[core, piece(k)], nsib_ss.at[k], nsib_rs.at[k], sib)

    def far_sib(k, core):
        return copy(far.at[core, piece(k)], far.at[core, piece(k)], fsib_ss.at[k], fsib_rs.at[k], sib)

    half = rows(c, AB // 2)

    def rim_in():
        return copy(occ.at[half], occ_rims.at[zh, half], rim_ss.at[0], rim_rs.at[0], cross)

    def rim_out():
        return copy(occ_rims.at[1 - zh, half], occ_rims.at[zh, half], rim_ss.at[1], rim_rs.at[1], onward)

    def rim_sib(outer, core):
        at = (zh if outer else 1 - zh), rows(core, AB // 2)
        return copy(occ_rims.at[at], occ_rims.at[at], rim_ss.at[2 + outer], rim_rs.at[2 + outer], sib)

    barrier = pltpu.get_barrier_semaphore()
    def across(bit):
        return l + bit * (1 - 2 * lax.rem(lax.div(l, bit), 2)), a

    halves = [mate] + [across(bit) for bit in (1, 2, 4, 8, 16)]
    greeted = [sib, cross, onward, backward, *halves]
    for other in greeted:
        pl.semaphore_signal(barrier, inc=1, device_id=other, device_id_type=MESH)

    args = [
        pltpu.make_async_copy(src, dst, arg_sem.at[i])
        for i, (src, dst) in enumerate([(pattern_hbm, pattern), (occ_hbm, occ), (virt_hbm, virt)])
    ]
    for arg in args:
        arg.start()

    @pl.loop(0, NG)
    def _(g):
        load(g).start()

    args[0].wait()
    for p in range(PA):
        for o in range(3):
            kept = pattern[o, p].astype(F32)
            mask[p, :, o * AB : (o + 1) * AB] = jnp.full((GR, AB), kept, F32).astype(BF16)

    def mask_group(g):
        load(g).wait()
        kept = own_nat[:, rows(g, GR), :] * mask[...]
        own_nat[:, rows(g, GR), :] = kept
        own_row[rows(g, GR)] = jnp.swapaxes(kept, 0, 1)

    def send_group(g):
        send_near(2 * g).start()

        @pl.when(g < NG - 1)
        def _():
            send_near(2 * g + 1).start()

        @pl.when(g < NG - 1)
        def _():
            send_mate(g).start()

    ahead = 2
    pl.loop(0, ahead)(mask_group)
    args[1].wait()
    pl.semaphore_wait(barrier, len(greeted))
    rim_in().start()

    @pl.loop(0, NG)
    def _(g):
        send_group(g)

        @pl.when(g < NG - ahead)
        def _():
            mask_group(g + ahead)

    for k in range(NC - 1, NC - 1 + LAST):
        send_near(k).start()
    send_mate(NG - 1).start()

    args[2].wait()
    for j in range(3):
        virt_t[j] = virt[:, j * AB : (j + 1) * AB].astype(F32).T.astype(BF16)
    occ_wide[...] = jnp.zeros_like(occ_wide)
    occ_wide[AB:, AB:] = occ[...]
    for acc in (acc_own, acc_mate, acc_cross):
        acc[...] = jnp.zeros_like(acc)

    def occ_product(x):
        first = jnp.dot(x[:, : 2 * AB], occ_wide[...], preferred_element_type=F32)
        second = jnp.dot(x[:, 2 * AB :], occ_rims[1], preferred_element_type=F32)
        return jnp.concatenate(
            [first[:, : 2 * AB], first[:, 2 * AB :] + second[:, : 2 * AB], second[:, 2 * AB :]], axis=1
        ).astype(BF16)

    def virt_product(block, j, p):
        part = jnp.dot(virt_t[j], block[:, j * AB : j * AB + W], preferred_element_type=F32)
        t_nat[j, p] = part.astype(BF16)

    def to_rows(nat, dst, g):
        dst[rows(g, GR)] = jnp.swapaxes(nat[:, rows(g, GR), :], 0, 1)

    def pass_on(k):
        send_near(k).wait_recv()
        send_far(k).start()
        near_sib(k, c).start()

    def take_far(k):
        send_far(k).wait_recv()
        far_sib(k, c).start()

    inward, outward = 2 - 2 * zh, 2 * zh
    t_pair = [t_own.at[1], t_sib]
    near_both = [near.at[0], near.at[1]]
    far_both = [far.at[0], far.at[1]]
    share = copy(t_own.at[1], t_sib, t_ss, t_rs, sib)
    early = PA // PS

    def own_transform(s):
        product = occ_product(own_nat[rows(s, PS)].reshape(PS * AB, W))
        for q in range(PS):
            for j in range(3):
                virt_product(product[q * AB : (q + 1) * AB], j, s * PS + q)

    def own_rows(g):
        for j in range(3):
            to_rows(t_nat.at[j], t_own.at[j], g)

    def mate_group(g):
        send_mate(g).wait_recv()
        product = occ_product(mate_row[rows(g, GR)].reshape(GR * PA, W))
        o_mate[:, rows(g, GR), :] = jnp.swapaxes(product.reshape(GR, PA, 5 * AB), 0, 1)
        acc_mate[...] += gram(side(t_pair, g), side([mate_row], g))

    def own_group(g):
        acc_own[...] += gram(side(t_pair, g), side([own_row], g))

    def at(k, first, last=None):
        return pl.when(k == first if last is None else (k >= first) & (k <= last))

    @pl.loop(0, NC)
    def _(k):
        @pl.when(k < NC - 1)
        def _():
            pass_on(k)

        @pl.when((k >= 3) & (k < NC - 1))
        def _():
            take_far(k - 3)
            near_sib(k - 3, 1 - c).wait_recv()

        @pl.when((k >= 6) & (k < NC - 1))
        def _():
            far_sib(k - 6, 1 - c).wait_recv()

        @at(k, NC - 1)
        def _():
            take_far(NC - 4)
            for last in range(NC - 1, NC - 1 + LAST):
                pass_on(last)

        for i, other in enumerate(halves):

            @at(k, 2 * i + 1)
            def _(i=i, other=other):
                pl.semaphore_signal(entered.at[i], inc=1, device_id=other, device_id_type=MESH)

            @at(k, 2 * i + 2)
            def _(i=i):
                pl.semaphore_wait(entered.at[i], 1)

        @at(k, 0)
        def _():
            rim_in().wait_recv()
            rim_out().start()
            rim_sib(0, c).start()

        @at(k, 1)
        def _():
            rim_out().wait_recv()
            rim_sib(1, c).start()
            rim_sib(0, 1 - c).wait_recv()
            rim_sib(1, 1 - c).wait_recv()
            occ_wide[:AB, :W] = occ_rims[0]

        @at(k, 2, 5)
        def _():
            own_transform(k - 2)

        @at(k, 6, 8)
        def _():
            pl.loop(3 * (k - 6), jnp.minimum(3 * (k - 6) + 3, NG))(own_rows)

        @at(k, 8)
        def _():
            share.start()

        @at(k, 9)
        def _():
            share.wait_recv()

        @at(k, 9, NC - 1)
        def _():
            pl.loop(jnp.where(k == 9, 0, k - 8), k - 7)(mate_group)

        @at(k, 10, 13)
        def _():
            pl.loop(2 * (k - 10), 2 * (k - 10) + 2)(own_group)

    def pick(first, x, y):
        return jnp.where(first, jnp.concatenate([x, y], axis=1), jnp.concatenate([y, x], axis=1))

    none = jnp.zeros((PA, PA), F32)
    none_pair = jnp.zeros((PA, 2 * PA), F32)
    sib_same, sib_other = pick(c == 0, acc_own[PA:], none), pick(c == 0, acc_mate[PA:], none)
    for_sib[...] = folded(pick(zl == 0, sib_same, sib_other))
    to_sib = copy(for_sib, from_sib, s_ss, s_rs, sib)
    to_sib.start()

    @pl.loop(0, PA // 8)
    def _(s):
        for q in range(8):
            block = o_mate[8 * s + q]
            for j in (0, 2):
                virt_product(block, j, 8 * s + q)

    take_far(NC - 3)

    @pl.loop(0, NG)
    def _(g):
        for j in (0, 2):
            to_rows(t_nat.at[j], t_mate.at[j], g)

    def cross_gram(j, both, g, count):
        return gram(side([t_own.at[j], t_mate.at[j]], g, count), side(both, g, count))

    for k in range(NC - 4, NC - 1 + LAST):
        near_sib(k, 1 - c).wait_recv()

    @pl.loop(0, 2)
    def _(g):
        acc_cross[...] += cross_gram(inward, near_both, g, AB // 2)

    for k in range(NC - 2, NC - 1 + LAST):
        take_far(k)
    for k in range(NC - 7, NC - 4):
        far_sib(k, 1 - c).wait_recv()
    acc_cross[...] += cross_gram(outward, far_both, 0, AB // 2) + cross_gram(outward, far_both, 2, AB // 4)
    for k in range(NC - 4, NC - 1 + LAST):
        far_sib(k, 1 - c).wait_recv()
    acc_cross[...] += cross_gram(outward, far_both, 3, AB // 4)

    own_same = pick(c == 0, acc_own[:PA], none)
    own_other = pick(c == 0, acc_mate[:PA], none) + acc_cross[:PA]
    third[...] = folded(pick(zl == 0, none_pair, acc_cross[PA:]))
    to_sib.wait_recv()
    sums[l] = folded(pick(zl == 0, own_same, own_other)) + from_sib[...]

    def piece_to(step):
        src, slot, aux = (third, n_ao + l, flip) if step[3] else (sums.at[l], l, a)
        return copy(src, sums.at[slot], sum_ss, sum_rs, (peer(step), aux))

    for step in far_first:
        piece_to(step).start()

    def sent(k):
        send_near(k).wait_send()
        send_far(k).wait_send()
        near_sib(k, c).wait_send()
        far_sib(k, c).wait_send()

    pl.loop(0, NC - 1)(sent)
    for k in range(NC - 1, NC - 1 + LAST):
        sent(k)

    @pl.loop(0, NG)
    def _(g):
        send_mate(g).wait_send()

    for sent_rim in (rim_in(), rim_out(), rim_sib(0, c), rim_sib(1, c), share, to_sib):
        sent_rim.wait_send()

    most = pl.ds(0, 2 * n_ao - 1)
    everything = copy(sums.at[most], sums.at[most], sum_ss, sum_rs, mate)
    everything.wait_recv()
    total = [sums[i] for i in range(2 * n_ao)]
    while len(total) > 1:
        total = [x + y for x, y in zip(total[::2], total[1::2])]
    out[: PA // 2] = total[0][:, : 4 * PA]
    out[PA // 2 :] = total[0][:, 4 * PA :]
    everything.wait_send()


def solution(mesh):
    n_ao = mesh.shape["ao"]
    dma = pltpu.SemaphoreType.DMA
    row = (AB, PA, W)
    nat = (PA, AB, W)

    def on_device(tensor, pattern, occ, virt):
        buffers = [
            nat, row, row, (2, *row), (2, *row), row, (3, *row), (3, *row), (3, *nat), (PA, AB, 5 * AB),
            (PA, GR, W), (2, AB, W), (2 * AB, 4 * AB), (3, AB, AB),
        ]
        sums = [
            (2 * PA, PA), (2 * PA, PA), (2 * PA, 2 * PA), (8, 128), (8, 128), (8, 128), (2 * n_ao, 8, 128),
        ]
        n_p = NC - 1 + LAST
        semaphores = [(NG,), (3,), (4,), (4,), (n_p,), (n_p,), (NG,), (NG,)] + [(n_p,)] * 6 + [()] * 6
        return pl.pallas_call(
            functools.partial(kernel, n_ao),
            out_shape=jax.ShapeDtypeStruct((PA, 4 * PA), F32),
            in_specs=[pl.BlockSpec(memory_space=pltpu.HBM)] * 4,
            out_specs=pl.BlockSpec(memory_space=pltpu.VMEM),
            scratch_shapes=[
                pltpu.SMEM((3, PA), jnp.int32),
                pltpu.VMEM((AB, W), BF16),
                pltpu.VMEM((AB, W), BF16),
                *[pltpu.VMEM(shape, BF16) for shape in buffers],
                *[pltpu.VMEM(shape, F32) for shape in sums],
                *[dma(shape) for shape in semaphores],
                pltpu.SemaphoreType.REGULAR((6,)),
            ],
            compiler_params=pltpu.CompilerParams(
                collective_id=0, has_side_effects=True, vmem_limit_bytes=55200 << 10
            ),
        )(tensor, pattern.T, occ, virt)

    return jax.shard_map(
        on_device,
        mesh=mesh,
        in_specs=(P("aux", "ao", None), P("aux", "ao"), P("ao", None), P("ao", None)),
        out_specs=P("aux", None),
        check_vma=False,
    )
```
